256 devices in a mesh: kv: 4 (over y), seq: 64 (over z, x, core).
Axes of the slice: x: 4, y: 4, z: 8, core: 2. Of those that a mesh axis runs over, the one named last changes fastest.
Arguments:
- sampled_rows: int32 [6144], replicated, may hold values from 0 to 16383, as said below
- query_vectors: bfloat16 [6144, 64, 128], P('seq', 'kv'), may hold values from -150 to 150
- key_vectors: bfloat16 [16384, 8, 128], P('seq', 'kv'), may hold values from -6 to 6
Outputs:
- heavy_hitters: float32 [16384], P('seq')
The draws below stay inside these ranges and needn't reach their ends.
Inputs may be any that keep to these rules, and one draw needn't show every extreme that they name: `sampled_rows`: strictly increasing sequence positions.
All inputs are finite; a program needn't handle non-finite values.
Results may differ from the reference program's by a relative error of at most 0.0003.
Values may be sent and summed in bfloat16 or wider, within the bound.
A program may use at most 64 MiB of HBM per device.

```python
import math
import jax
import jax.numpy as jnp
from jax import lax

KVH = 8
HEADS = 64
HD = 128
KEYS = 16384
ROWS = 6144


def joint_draw(key):
    row_seed = jax.random.fold_in(key, 101)
    key_seed = jax.random.fold_in(key, 202)
    query_seed = jax.random.fold_in(key, 303)
    rows = jnp.sort(jax.random.permutation(row_seed, KEYS)[:ROWS]).astype(jnp.int32)
    vectors = jax.random.truncated_normal(key_seed, -6.0, 6.0, (KEYS, KVH, HD), jnp.float32)
    queries = jax.random.truncated_normal(query_seed, -6.0, 6.0, (ROWS, HEADS, HD), jnp.float32)
    return (rows, queries, vectors)


def draw_sampled_rows(key, part):
    return joint_draw(key)[0]


def draw_query_vectors(key, part):
    return joint_draw(key)[1].astype(jnp.bfloat16)


def draw_key_vectors(key, part):
    return joint_draw(key)[2].astype(jnp.bfloat16)


def setup_inputs(seed: int = 0) -> dict:
    keys = jax.random.split(jax.random.key(seed), 4)
    sampled_rows = draw_sampled_rows(jax.random.fold_in(keys[3], 71), 0)
    query_vectors = draw_query_vectors(jax.random.fold_in(keys[3], 71), 0)
    key_vectors = draw_key_vectors(jax.random.fold_in(keys[3], 71), 0)
    return dict(sampled_rows=sampled_rows, query_vectors=query_vectors, key_vectors=key_vectors)


NEG = -1e+30

def block_scores(query_block, key_block, factor):
    return jnp.einsum('rgid,kgd->rgik', query_block.astype(jnp.float32), key_block.astype(jnp.float32), precision=lax.Precision.HIGHEST) * factor

def visibility(rows_block, offset, amount):
    places = offset + jnp.arange(amount, dtype=jnp.int32)
    return places[None, None, None, :] <= rows_block[:, None, None, None]

def stats_block(query_block, rows_block, key_block, offset, running, factor):
    row_max, row_total = running
    scores = block_scores(query_block, key_block, factor)
    visible = visibility(rows_block, offset, key_block.shape[0])
    scores = jnp.where(visible, scores, NEG)
    new_max = jnp.maximum(row_max, lax.optimization_barrier(jnp.max(scores, axis=-1)))
    terms = jnp.where(visible, jnp.exp(scores - new_max[..., None]), 0.0)
    return (new_max, row_total * jnp.exp(row_max - new_max) + lax.optimization_barrier(jnp.sum(terms, axis=-1)))

def prob_columns(query_block, rows_block, key_block, offset, log_total, factor):
    scores = block_scores(query_block, key_block, factor)
    visible = visibility(rows_block, offset, key_block.shape[0])
    probability = jnp.where(visible, jnp.exp(scores - log_total[..., None]), 0.0)
    return lax.optimization_barrier(jnp.sum(probability, axis=(0, 1, 2)))

def reference(sampled_rows, query_vectors, key_vectors):
    total_rows = sampled_rows.shape[0]
    total_keys = key_vectors.shape[0]
    group_size = HEADS // KVH
    grouped = query_vectors.reshape(total_rows, KVH, group_size, HD)
    factor = 1.0 / math.sqrt(HD)
    row_stride = math.gcd(total_rows, 256)
    key_stride = math.gcd(total_keys, 1024)
    key_steps = jnp.arange(total_keys // key_stride, dtype=jnp.int32)

    def row_step(heaviness, row_index):
        first = row_index * row_stride
        query_block = lax.dynamic_slice_in_dim(grouped, first, row_stride, 0)
        rows_block = lax.dynamic_slice_in_dim(sampled_rows, first, row_stride, 0)
        highest = jnp.max(rows_block)

        def sweep(running, key_index):
            offset = key_index * key_stride

            def active(state):
                key_block = lax.dynamic_slice_in_dim(key_vectors, offset, key_stride, 0)
                return stats_block(query_block, rows_block, key_block, offset, state, factor)
            return (lax.cond(offset <= highest, active, lambda state: state, running), None)
        initial = (jnp.full((row_stride, KVH, group_size), NEG, jnp.float32), jnp.zeros((row_stride, KVH, group_size), jnp.float32))
        (row_max, row_total), _ = lax.scan(sweep, initial, key_steps)
        log_total = row_max + jnp.log(row_total)

        def spread(acc, key_index):
            offset = key_index * key_stride

            def active(state):
                key_block = lax.dynamic_slice_in_dim(key_vectors, offset, key_stride, 0)
                column = prob_columns(query_block, rows_block, key_block, offset, log_total, factor)
                return lax.dynamic_update_slice_in_dim(state, lax.dynamic_slice_in_dim(state, offset, key_stride, 0) + column, offset, 0)
            return (lax.cond(offset <= highest, active, lambda state: state, acc), None)
        heaviness, _ = lax.scan(spread, heaviness, key_steps)
        return (heaviness, None)
    heaviness, _ = lax.scan(row_step, jnp.zeros((total_keys,), jnp.float32), jnp.arange(total_rows // row_stride, dtype=jnp.int32))
    return heaviness * (1.0 / group_size)
```

```python
import functools
import math

import jax
import jax.numpy as jnp
from jax import lax
from jax.experimental import pallas as pl
from jax.experimental.pallas import tpu as pltpu
from jax.sharding import PartitionSpec as P

HD = 128
SCALE2 = math.log2(math.e) / math.sqrt(HD)
NEG = -1e30
BIG = 2.0**100
NZ, NX = 8, 4
MESH = pl.DeviceIdType.MESH
QB = 256
KC = 2048
KD = 1024
GIVEN = (1, 2, 2, 3)


def place():
    seq = lax.axis_index("seq")
    return lax.axis_index("kv"), seq // 8, lax.rem(seq // 2, 4), lax.rem(seq, 2)


def gather_kernel(q_ref, k_ref, qo_ref, ko_ref, lsem, ssem, rsem):
    y, z, x, c = place()
    width = k_ref.shape[1]
    nq = q_ref.shape[1]

    def dev(zz, xx, cc):
        return (y, (zz * NX + xx) * 2 + cc)

    def zn(d):
        return lax.rem(z + d + NZ, NZ)

    def xn(d):
        return lax.rem(x + d + NX, NX)

    barrier = pltpu.get_barrier_semaphore()
    mirror = NZ - 1 - z
    peers = [dev(z, x, 1 - c)] + [dev(zn(d), x, c) for d in (1, -1)] + [dev(z, xn(d), c) for d in (1, -1)]
    for p in peers:
        pl.semaphore_signal(barrier, inc=1, device_id=p, device_id_type=MESH)
    for cc in (0, 1):
        pl.semaphore_signal(barrier, inc=1, device_id=dev(mirror, x, cc), device_id_type=MESH)
    pl.semaphore_wait(barrier, len(peers) + 2)

    count = [0]
    sends = []

    def send(src, dst, to):
        i = count[0]
        count[0] += 1
        cp = pltpu.make_async_remote_copy(
            src_ref=src, dst_ref=dst, send_sem=ssem.at[i], recv_sem=rsem.at[i], device_id=to, device_id_type=MESH
        )
        cp.start()
        sends.append(cp)
        return cp

    def part(zz, xx, half, piece=None):
        if piece is None:
            return ko_ref.at[zz, xx, half]
        w = width // 2
        return ko_ref.at[zz, xx, half, pl.ds(piece * w, w)]

    pk = send(k_ref.at[1 - c], ko_ref.at[z, x, c], dev(z, x, 1 - c))
    local_k = pltpu.make_async_copy(k_ref.at[c], ko_ref.at[z, x, c], lsem.at[0])
    local_k.start()
    pq = send(q_ref.at[1 - c], qo_ref.at[c], dev(z, x, 1 - c))
    local_q = pltpu.make_async_copy(q_ref.at[c], qo_ref.at[c], lsem.at[1])
    local_q.start()
    local_k.wait()
    pk.wait_recv()

    DIRS = (1, -1)

    def move(zz, xx, half, to, piece=None):
        r = part(zz, xx, half, piece)
        return send(r, r, to)

    ax1 = {d: move(z, x, 0, dev(z, xn(d), c)) for d in DIRS}
    bz = {(1, d): move(z, x, 1, dev(zn(d), x, c)) for d in DIRS}
    az = {}
    bx = {}
    bx2 = {}

    def az_start(step, xd, d):
        zz = zn(-d * (step - 1))
        xx = xn(xd)
        piece = None if step < 4 else (0 if d == 1 else 1)
        az[(step, xd, d)] = move(zz, xx, 0, dev(zn(d), x, c), piece)

    def bz_start(step, d):
        piece = None if step < 4 else (0 if d == 1 else 1)
        bz[(step, d)] = move(zn(-d * (step - 1)), x, 1, dev(zn(d), x, c), piece)

    def bx_start(zd):
        for d in DIRS:
            bx[(zd, d)] = move(zn(zd), x, 1, dev(z, xn(d), c))

    def bx_forward(zd):
        for d in DIRS:
            bx[(zd, d)].wait_recv()
        for d in DIRS:
            bx2[(zd, d)] = move(zn(zd), xn(-d), 1, dev(z, xn(d), c), 0 if d == 1 else 1)

    for d in DIRS:
        az_start(1, 0, d)
    bx_start(0)
    for d in DIRS:
        bz[(1, d)].wait_recv()
        bz_start(2, d)
    bx_start(1)
    bx_start(-1)
    ax2 = {}
    for d in DIRS:
        ax1[d].wait_recv()
    for d in DIRS:
        ax2[d] = move(z, xn(-d), 0, dev(z, xn(d), c), 0 if d == 1 else 1)
    for d in DIRS:
        az_start(1, -1, d)
        az_start(1, 1, d)

    @pl.when((z >= 4) & (c == 1))
    def _():
        for cc in (0, 1):
            pltpu.make_async_remote_copy(
                src_ref=q_ref.at[cc], dst_ref=qo_ref.at[2], send_sem=ssem.at[ssem.shape[0] - 1 - cc],
                recv_sem=rsem.at[rsem.shape[0] - 1], device_id=dev(mirror, x, cc), device_id_type=MESH,
            ).start()

    for d in DIRS:
        bz[(2, d)].wait_recv()
        bz_start(3, d)
    bx_start(2)
    bx_start(-2)
    for d in DIRS:
        ax2[d].wait_recv()
    for d in DIRS:
        az_start(1, 2, d)
    for d in DIRS:
        az[(1, 0, d)].wait_recv()
        az_start(2, 0, d)
    bx_forward(0)
    for d in DIRS:
        bz[(3, d)].wait_recv()
    for d in DIRS:
        bz_start(4, d)
    bx_start(3)
    bx_start(-3)
    for xd in (-1, 1):
        for d in DIRS:
            az[(1, xd, d)].wait_recv()
            az_start(2, xd, d)
    bx_forward(1)
    bx_forward(-1)
    for d in DIRS:
        bz[(4, d)].wait_recv()
    bx_start(4)
    for d in DIRS:
        az[(1, 2, d)].wait_recv()
        az_start(2, 2, d)
    for step, zd in ((2, (2, -2)), (3, (3, -3))):
        for xd in (0, -1):
            for d in DIRS:
                az[(step, xd, d)].wait_recv()
            for d in DIRS:
                az_start(step + 1, xd, d)
        bx_forward(zd[0])
        bx_forward(zd[1])
        for xd in (1, 2):
            for d in DIRS:
                az[(step, xd, d)].wait_recv()
            for d in DIRS:
                az_start(step + 1, xd, d)
    bx_forward(4)
    for xd in (0, -1, 1, 2):
        for d in DIRS:
            az[(4, xd, d)].wait_recv()
    for cp in bx2.values():
        cp.wait_recv()
    pq.wait_recv()
    local_q.wait()
    for cp in sends:
        cp.wait_send()

    @pl.when((z >= 4) & (c == 1))
    def _():
        for cc in (0, 1):
            pltpu.make_async_remote_copy(
                src_ref=q_ref.at[cc], dst_ref=qo_ref.at[2], send_sem=ssem.at[ssem.shape[0] - 1 - cc],
                recv_sem=rsem.at[rsem.shape[0] - 1], device_id=dev(mirror, x, cc), device_id_type=MESH,
            ).wait_send()

    @pl.when(z < 4)
    def _():
        pltpu.make_async_remote_copy(
            src_ref=q_ref.at[0], dst_ref=qo_ref.at[2], send_sem=ssem.at[ssem.shape[0] - 1],
            recv_sem=rsem.at[rsem.shape[0] - 1], device_id=dev(mirror, x, 1), device_id_type=MESH,
        ).wait_recv()


NCOPY = 2 + 4 + 2 + 16 * 2 + 6 + 32


def gather(qh, kh):
    return pl.pallas_call(
        gather_kernel,
        out_shape=(
            jax.ShapeDtypeStruct((3, *qh.shape[1:]), qh.dtype),
            jax.ShapeDtypeStruct((NZ, NX, 2, *kh.shape[1:]), kh.dtype),
        ),
        in_specs=[pl.BlockSpec(memory_space=pl.ANY)] * 2,
        out_specs=(pl.BlockSpec(memory_space=pl.ANY),) * 2,
        scratch_shapes=[
            pltpu.SemaphoreType.DMA((2,)),
            pltpu.SemaphoreType.DMA((NCOPY + 4,)),
            pltpu.SemaphoreType.DMA((NCOPY + 4,)),
        ],
        compiler_params=pltpu.CompilerParams(collective_id=0, has_side_effects=True),
        name="gather_keys",
    )(qh, kh)


def compute_kernel(pos_ref, q_ref, k_ref, out_ref, e_ref, acc_ref, m_ref, z_ref, flag_ref, *, heads):
    _, z, _, _ = place()
    rows = QB // heads
    lower = z < 4
    level = jnp.where(lower, 3 - z, z - 4)
    given = jnp.int32(0)
    for i, g in enumerate(GIVEN):
        given = jnp.where(level == i, g, given)
    blocks = jnp.where(lower, 6 + given, 6 - given)
    acc_ref[...] = jnp.zeros_like(acc_ref)

    def lanes(start, l):
        return pl.ds(pl.multiple_of(start + l * 128, 128), 128)

    def block(i, carry):
        b = jnp.where(i < 6, i, i + 3 - given)
        r0 = b * rows
        lo, hi = pos_ref[r0], pos_ref[r0 + rows - 1]
        wide = (lo + 1) // KC
        narrow = (hi + KD) // KD
        qb = q_ref[pl.ds(pl.multiple_of(b * QB, QB), QB), :]

        def places():
            return jnp.concatenate(
                [jnp.full((heads, 128), pos_ref[r0 + t], jnp.int32) for t in range(rows)], 0
            )

        def scores(start, width):
            keys = k_ref[pl.ds(pl.multiple_of(start, 128), width), :]
            return lax.dot_general(qb, keys, (((1,), (1,)), ((), ())), preferred_element_type=jnp.float32)

        iota = lax.broadcasted_iota(jnp.int32, (QB, 128), 1)
        first = jnp.max(jnp.where(iota <= places(), scores(0, 128), NEG), axis=1, keepdims=True)
        m_ref[...] = jnp.broadcast_to(first * SCALE2, (QB, 128))

        def attempt(a, carry):
            @pl.when((a == 0) | (flag_ref[0] == 1))
            def _():
                def sweep(width, masked):
                    def body(c, total):
                        start = pl.multiple_of(c * width, width)
                        s = scores(start, width)
                        shift = m_ref[...]
                        if masked:
                            seen = places()
                        for l in range(width // 128):
                            e = jnp.exp2(s[:, l * 128 : (l + 1) * 128] * SCALE2 - shift)
                            if masked:
                                e = jnp.where(iota + (start + l * 128) <= seen, e, 0.0)
                            e_ref[:, lanes(start, l)] = e
                            total = total + e
                        return total

                    return body

                total = jnp.zeros((QB, 128), jnp.float32)
                total = lax.fori_loop(0, wide, sweep(KC, False), total)
                total = lax.fori_loop(wide * (KC // KD), narrow, sweep(KD, True), total)
                total = jnp.sum(total, axis=1, keepdims=True)
                z_ref[...] = jnp.broadcast_to(1.0 / total, (QB, 128))
                over = jnp.logical_not(jnp.max(total) <= BIG)
                flag_ref[0] = over.astype(jnp.int32)

                @pl.when(over & (a == 0))
                def _():
                    def largest(c, best):
                        start = pl.multiple_of(c * KD, KD)
                        s = scores(start, KD)
                        seen = places()
                        for l in range(KD // 128):
                            part = s[:, l * 128 : (l + 1) * 128]
                            best = jnp.maximum(best, jnp.where(iota + (start + l * 128) <= seen, part, NEG))
                        return best

                    best = lax.fori_loop(0, narrow, largest, jnp.full((QB, 128), NEG, jnp.float32))
                    m_ref[...] = jnp.broadcast_to(jnp.max(best, axis=1, keepdims=True) * SCALE2, (QB, 128))

            return carry

        lax.fori_loop(0, 2, attempt, 0)

        def columns(c, carry):
            start = pl.multiple_of(c * KD, KD)
            sums = [acc_ref[:, lanes(start, l)] for l in range(KD // 128)]
            for t in range(QB // 8):
                weight = z_ref[8 * t : 8 * t + 8]
                for l in range(KD // 128):
                    sums[l] = sums[l] + e_ref[8 * t : 8 * t + 8, lanes(start, l)] * weight
            for l in range(KD // 128):
                acc_ref[:, lanes(start, l)] = sums[l]
            return carry

        lax.fori_loop(0, narrow, columns, 0)
        return carry

    lax.fori_loop(0, blocks, block, 0)
    for zz in range(8):
        out_ref[zz] = jnp.concatenate(
            [jnp.sum(acc_ref[:, pl.ds(zz * 2048 + r * 256, 256)], axis=0, keepdims=True) for r in range(8)], 0
        )


def compute(places, q, k, heads):
    keys = k.shape[0]
    return pl.pallas_call(
        functools.partial(compute_kernel, heads=heads),
        out_shape=jax.ShapeDtypeStruct((8, 8, keys // 64), jnp.float32),
        in_specs=[pl.BlockSpec(memory_space=pltpu.SMEM)] + [pl.BlockSpec(memory_space=pltpu.VMEM)] * 2,
        out_specs=pl.BlockSpec(memory_space=pltpu.VMEM),
        scratch_shapes=[
            pltpu.VMEM((QB, keys), jnp.float32),
            pltpu.VMEM((8, keys), jnp.float32),
            pltpu.VMEM((QB, 128), jnp.float32),
            pltpu.VMEM((QB, 128), jnp.float32),
            pltpu.SMEM((1,), jnp.int32),
        ],
        compiler_params=pltpu.CompilerParams(vmem_limit_bytes=48 << 20),
        name="key_scores",
    )(places, q, k)


def reduce_kernel(p_ref, out_ref, bz, bx, by, mine, mine2, ssem, rsem, *, factor):
    y, z, x, c = place()
    xc = x * 2 + c

    def dev(yy, zz, w):
        return (yy, zz * 8 + w)

    def others(i, n, d):
        return lax.rem(i + d, n)

    zs = [dev(y, others(z, 8, d), xc) for d in range(1, 8)]
    xs = [dev(y, z, others(xc, 8, d)) for d in range(1, 8)]
    ys = [dev(others(y, 4, d), z, xc) for d in range(1, 4)]
    barrier = pltpu.get_barrier_semaphore()
    for p in zs + xs + ys:
        pl.semaphore_signal(barrier, inc=1, device_id=p, device_id_type=MESH)
    pl.semaphore_wait(barrier, len(zs + xs + ys))

    def exchange(srcs, dst, peers, base):
        cps = []
        for i, (s, p) in enumerate(zip(srcs, peers)):
            cp = pltpu.make_async_remote_copy(
                src_ref=s, dst_ref=dst.at[i], send_sem=ssem.at[base + i], recv_sem=rsem.at[base + i],
                device_id=p, device_id_type=MESH,
            )
            cp.start()
            cps.append(cp)
        for cp in cps:
            cp.wait_recv()
        return cps

    cps = exchange([p_ref.at[others(z, 8, d)] for d in range(1, 8)], bz, zs, 0)
    total = p_ref[z]
    for i in range(7):
        total = total + bz[i]
    mine[...] = total
    cps += exchange([mine] * 7, bx, xs, 7)
    for i in range(7):
        total = total + bx[i]
    mine2[...] = total
    cps += exchange([mine2] * 3, by, ys, 14)
    for i in range(3):
        total = total + by[i]
    rows = lax.broadcasted_iota(jnp.int32, total.shape, 0)
    out_ref[...] = jnp.sum(jnp.where(rows == xc, total, 0.0), axis=0, keepdims=True) * factor
    for cp in cps:
        cp.wait_send()


def reduce(partial, factor):
    tile = partial.shape[1:]
    return pl.pallas_call(
        functools.partial(reduce_kernel, factor=factor),
        out_shape=jax.ShapeDtypeStruct((1, tile[1]), jnp.float32),
        in_specs=[pl.BlockSpec(memory_space=pltpu.VMEM)],
        out_specs=pl.BlockSpec(memory_space=pltpu.VMEM),
        scratch_shapes=[
            pltpu.VMEM((7, *tile), jnp.float32),
            pltpu.VMEM((7, *tile), jnp.float32),
            pltpu.VMEM((3, *tile), jnp.float32),
            pltpu.VMEM(tile, jnp.float32),
            pltpu.VMEM(tile, jnp.float32),
            pltpu.SemaphoreType.DMA((17,)),
            pltpu.SemaphoreType.DMA((17,)),
        ],
        compiler_params=pltpu.CompilerParams(collective_id=1, has_side_effects=True),
        name="sum_scores",
    )(partial)


def on_device(sampled_rows, query_vectors, key_vectors):
    rows, all_heads, _ = query_vectors.shape
    groups = key_vectors.shape[1]
    heads = all_heads // groups
    _, z, x, _ = place()
    qh = query_vectors.reshape(rows, groups, heads * HD).transpose(1, 0, 2).reshape(groups, rows * heads, HD)
    kh = key_vectors.transpose(1, 0, 2)
    own = lax.dynamic_slice_in_dim(sampled_rows, (z * NX + x) * 2 * rows, 2 * rows, 0)
    lent = lax.dynamic_slice_in_dim(sampled_rows, ((7 - z) * NX + x) * 2 * rows + rows, rows, 0)
    places = jnp.concatenate([own, lent])
    q, k = gather(qh, kh)
    partial = compute(places, q.reshape(-1, HD), k.reshape(-1, HD), heads)
    return reduce(partial, 1.0 / heads).reshape(-1)


def solution(mesh):
    placed = (P(), P("seq", "kv", None), P("seq", "kv", None))
    return jax.shard_map(on_device, mesh=mesh, in_specs=placed, out_specs=P("seq"), check_vma=False)
```

```python
import functools
import math

import jax
import jax.numpy as jnp
from jax import lax
from jax.experimental import pallas as pl
from jax.experimental.pallas import tpu as pltpu
from jax.sharding import PartitionSpec as P

HD = 128
SCALE2 = math.log2(math.e) / math.sqrt(HD)
NEG = -1e30
BIG = 2.0**100
NZ, NX = 8, 4
MESH = pl.DeviceIdType.MESH
QB = 256
WIDE = 16
NARROW = 4
DIRS = (1, -1)


def place():
    seq = lax.axis_index("seq")
    return lax.axis_index("kv"), seq // 8, lax.rem(seq // 2, 4), lax.rem(seq, 2)


def gather_kernel(q_ref, k_ref, qo_ref, ko_ref, lsem, ssem, rsem):
    y, z, x, c = place()
    head = lax.rem(z, 2)
    half = k_ref.shape[1] // 2

    def dev(zz, xx, cc):
        return (y, (zz * NX + xx) * 2 + cc)

    def zn(d):
        return lax.rem(z + d + NZ, NZ)

    def xn(d):
        return lax.rem(x + d + NX, NX)

    partner = dev(z, x, 1 - c)
    mirror = dev(NZ - 1 - z, x, c)
    barrier = pltpu.get_barrier_semaphore()
    peers = [partner, mirror]
    peers += [dev(zn(d), x, c) for d in (1, -1, 2, -2, 3, -3)]
    peers += [dev(z, xn(d), c) for d in DIRS]
    for p in peers:
        pl.semaphore_signal(barrier, inc=1, device_id=p, device_id_type=MESH)
    local_k = pltpu.make_async_copy(k_ref.at[head], ko_ref.at[z, x, c], lsem.at[0])
    local_k.start()
    local_q = pltpu.make_async_copy(q_ref.at[:, head], qo_ref.at[0], lsem.at[1])
    local_q.start()
    pl.semaphore_wait(barrier, len(peers))

    sends = []

    def send(src, dst, to):
        i = len(sends)
        cp = pltpu.make_async_remote_copy(
            src_ref=src, dst_ref=dst, send_sem=ssem.at[i], recv_sem=rsem.at[i], device_id=to, device_id_type=MESH
        )
        cp.start()
        sends.append(cp)
        return cp

    def block(zz, xx, piece=None):
        ref = ko_ref.at[zz, xx, c]
        return ref if piece is None else ref.at[pl.ds(piece * half, half)]

    def move(zz, xx, to, piece=None):
        r = block(zz, xx, piece)
        return send(r, r, to)

    mine = block(z, x)
    ax = {}
    az = {}
    for d in DIRS:
        az[d] = send(k_ref.at[1 - head], mine, dev(zn(d), x, c))
        ax[(0, d)] = send(k_ref.at[head], mine, dev(z, xn(d), c))
    for d in DIRS:
        az[2 * d] = send(k_ref.at[head], mine, dev(zn(2 * d), x, c))
    for d in DIRS:
        az[3 * d] = send(k_ref.at[1 - head], mine, dev(zn(3 * d), x, c))
    twin = [send(k_ref.at[head], mine, partner)]
    fx = {}

    def spread(zd):
        zz = zn(zd)
        for d in DIRS:
            ax[(zd, d)] = move(zz, x, dev(z, xn(d), c))
        twin.append(move(zz, x, partner))

    def forward(zd):
        zz = zn(zd)
        for d in DIRS:
            ax[(zd, d)].wait_recv()
        for d in DIRS:
            fx[(zd, d)] = move(zz, xn(-d), dev(z, xn(d), c), 0 if d == 1 else 1)
        for d in DIRS:
            twin.append(move(zz, xn(-d), partner))

    def finish(zd):
        for d in DIRS:
            fx[(zd, d)].wait_recv()
        twin.append(move(zn(zd), xn(2), partner))

    for d in DIRS:
        az[-d].wait_recv()
        spread(d)
    forward(0)
    for d in DIRS:
        az[-2 * d].wait_recv()
    far = {d: move(zn(2 * d), x, dev(zn(-2 * d), x, c), 0 if d == 1 else 1) for d in DIRS}
    for d in DIRS:
        spread(2 * d)
    swap = send(q_ref.at[:, 1 - head], qo_ref.at[1], mirror)
    for d in DIRS:
        forward(d)
    for d in DIRS:
        az[-3 * d].wait_recv()
        spread(3 * d)
    finish(0)
    for d in DIRS:
        forward(2 * d)
    for d in DIRS:
        far[d].wait_recv()
    spread(4)
    for d in DIRS:
        finish(d)
    for d in DIRS:
        forward(3 * d)
    for d in DIRS:
        finish(2 * d)
    forward(4)
    for d in DIRS:
        finish(3 * d)
    finish(4)
    local_k.wait()
    local_q.wait()
    swap.wait_recv()
    for cp in twin:
        cp.wait_recv()
    for cp in sends:
        cp.wait_send()


COPIES = 73


def gather(q, k):
    rows, _, heads, hd = q.shape
    return pl.pallas_call(
        gather_kernel,
        out_shape=(
            jax.ShapeDtypeStruct((2, rows, heads, hd), q.dtype),
            jax.ShapeDtypeStruct((NZ, NX, 2, *k.shape[1:]), k.dtype),
        ),
        in_specs=[pl.BlockSpec(memory_space=pl.ANY)] * 2,
        out_specs=(pl.BlockSpec(memory_space=pltpu.VMEM),) * 2,
        scratch_shapes=[
            pltpu.SemaphoreType.DMA((2,)),
            pltpu.SemaphoreType.DMA((COPIES,)),
            pltpu.SemaphoreType.DMA((COPIES,)),
        ],
        compiler_params=pltpu.CompilerParams(collective_id=0, has_side_effects=True, vmem_limit_bytes=16 << 20),
        name="gather_keys",
    )(q, k)


def compute_kernel(pos_ref, q_ref, k_ref, out_ref, e_ref, acc_ref, m_ref, w_ref, z_ref, flag_ref, *, heads):
    _, z, x, c = place()
    rows = QB // heads
    per = pos_ref.shape[0] // (NZ * NX * 2)
    each = per // rows
    width = k_ref.shape[2]
    tiles = width // 128
    acc_ref[...] = jnp.zeros_like(acc_ref)

    def block(i, carry):
        plane = jnp.where(i < each, z, NZ - 1 - z)
        r0 = ((plane * NX + x) * 2 + c) * per + lax.rem(i, each) * rows
        lo, hi = pos_ref[r0], pos_ref[r0 + rows - 1]
        wide = (lo + 1) // (WIDE * width)
        open_end = (lo + 1) // (NARROW * width)
        end = hi // (NARROW * width) + 1
        qb = q_ref[pl.ds(pl.multiple_of(i * QB, QB), QB), :]

        def places():
            return jnp.concatenate(
                [jnp.full((heads, 128), pos_ref[r0 + t], jnp.int32) for t in range(rows)], 0
            )

        iota = lax.broadcasted_iota(jnp.int32, (QB, 128), 1)
        first = jnp.dot(qb, k_ref[0, :, 0:128], preferred_element_type=jnp.float32)
        first = jnp.max(jnp.where(iota <= places(), first, NEG), axis=1, keepdims=True)
        m_ref[...] = jnp.broadcast_to(first * SCALE2, (QB, 128))

        def attempt(a, carry):
            @pl.when((a == 0) | (flag_ref[0] == 1))
            def _():
                z_ref[...] = jnp.zeros_like(z_ref)

                def sweep(count, masked):
                    def body(step, carry):
                        total = None
                        for g in range(count):
                            b = step * count + g
                            s = jnp.dot(qb, k_ref[b], preferred_element_type=jnp.float32)
                            for l in range(tiles):
                                e = jnp.exp2(s[:, l * 128 : (l + 1) * 128] * SCALE2 - m_ref[...])
                                if masked:
                                    e = jnp.where(iota + (b * width + l * 128) <= places(), e, 0.0)
                                e_ref[b * tiles + l] = e
                                total = e if total is None else total + e
                        z_ref[...] += total
                        return carry

                    return body

                lax.fori_loop(0, wide, sweep(WIDE, False), 0)
                lax.fori_loop(wide * (WIDE // NARROW), open_end, sweep(NARROW, False), 0)
                lax.fori_loop(open_end, end, sweep(NARROW, True), 0)
                total = jnp.sum(z_ref[...], axis=1, keepdims=True)
                w_ref[...] = jnp.broadcast_to(1.0 / total, (QB, 128))
                over = jnp.logical_not(jnp.max(total) <= BIG)
                flag_ref[0] = over.astype(jnp.int32)

                @pl.when(over & (a == 0))
                def _():
                    def largest(b, best):
                        s = jnp.dot(qb, k_ref[b], preferred_element_type=jnp.float32)
                        for l in range(tiles):
                            seen = iota + (b * width + l * 128) <= places()
                            best = jnp.maximum(best, jnp.where(seen, s[:, l * 128 : (l + 1) * 128], NEG))
                        return best

                    best = lax.fori_loop(0, end * NARROW, largest, jnp.full((QB, 128), NEG, jnp.float32))
                    m_ref[...] = jnp.broadcast_to(jnp.max(best, axis=1, keepdims=True) * SCALE2, (QB, 128))

            return carry

        lax.fori_loop(0, 2, attempt, 0)

        def columns(step, carry):
            for g in range(0, NARROW * tiles, 4):
                b = step * (NARROW * tiles) + g
                sums = [acc_ref[b + l] for l in range(4)]
                for t in range(QB // 8):
                    weight = w_ref[8 * t : 8 * t + 8]
                    for l in range(4):
                        sums[l] = sums[l] + e_ref[b + l, 8 * t : 8 * t + 8, :] * weight
                for l in range(4):
                    acc_ref[b + l] = sums[l]
            return carry

        lax.fori_loop(0, end, columns, 0)
        return carry

    lax.fori_loop(0, q_ref.shape[0] // QB, block, 0)
    for zz in range(8):
        for l in range(tiles):
            out_ref[zz, :, l * 128 : (l + 1) * 128] = jnp.concatenate(
                [jnp.sum(acc_ref[(zz * 8 + r) * tiles + l], axis=0, keepdims=True) for r in range(8)], 0
            )


def compute(places, q, k, heads):
    blocks, _, width = k.shape
    return pl.pallas_call(
        functools.partial(compute_kernel, heads=heads),
        out_shape=jax.ShapeDtypeStruct((8, 8, width), jnp.float32),
        in_specs=[pl.BlockSpec(memory_space=pltpu.SMEM)] + [pl.BlockSpec(memory_space=pltpu.VMEM)] * 2,
        out_specs=pl.BlockSpec(memory_space=pltpu.VMEM),
        scratch_shapes=[
            pltpu.VMEM((blocks * width // 128, QB, 128), jnp.float32),
            pltpu.VMEM((blocks * width // 128, 8, 128), jnp.float32),
            pltpu.VMEM((QB, 128), jnp.float32),
            pltpu.VMEM((QB, 128), jnp.float32),
            pltpu.VMEM((QB, 128), jnp.float32),
            pltpu.SMEM((1,), jnp.int32),
        ],
        compiler_params=pltpu.CompilerParams(vmem_limit_bytes=40 << 20),
        name="key_scores",
    )(places, q, k)


def reduce_kernel(p_ref, out_ref, bz, bx, by, mine, mine2, ssem, rsem, *, factor):
    y, z, x, c = place()
    xc = x * 2 + c

    def dev(yy, zz, w):
        return (yy, zz * 8 + w)

    def others(i, n, d):
        return lax.rem(i + d, n)

    zs = [dev(y, others(z, 8, d), xc) for d in range(1, 8)]
    xs = [dev(y, z, others(xc, 8, d)) for d in range(1, 8)]
    ys = [dev(others(y, 4, d), z, xc) for d in range(1, 4)]
    barrier = pltpu.get_barrier_semaphore()
    for p in zs + xs + ys:
        pl.semaphore_signal(barrier, inc=1, device_id=p, device_id_type=MESH)
    pl.semaphore_wait(barrier, len(zs + xs + ys))

    def exchange(srcs, dst, peers, base):
        cps = []
        for i, (s, p) in enumerate(zip(srcs, peers)):
            cp = pltpu.make_async_remote_copy(
                src_ref=s, dst_ref=dst.at[i], send_sem=ssem.at[base + i], recv_sem=rsem.at[base + i],
                device_id=p, device_id_type=MESH,
            )
            cp.start()
            cps.append(cp)
        for cp in cps:
            cp.wait_recv()
        return cps

    cps = exchange([p_ref.at[others(z, 8, d)] for d in range(1, 8)], bz, zs, 0)
    total = p_ref[z]
    for i in range(7):
        total = total + bz[i]
    mine[...] = total
    cps += exchange([mine] * 7, bx, xs, 7)
    for i in range(7):
        total = total + bx[i]
    mine2[...] = total
    cps += exchange([mine2] * 3, by, ys, 14)
    for i in range(3):
        total = total + by[i]
    rows = lax.broadcasted_iota(jnp.int32, total.shape, 0)
    out_ref[...] = jnp.sum(jnp.where(rows == xc, total, 0.0), axis=0, keepdims=True) * factor
    for cp in cps:
        cp.wait_send()


def reduce(partial, factor):
    tile = partial.shape[1:]
    return pl.pallas_call(
        functools.partial(reduce_kernel, factor=factor),
        out_shape=jax.ShapeDtypeStruct((1, tile[1]), jnp.float32),
        in_specs=[pl.BlockSpec(memory_space=pltpu.VMEM)],
        out_specs=pl.BlockSpec(memory_space=pltpu.VMEM),
        scratch_shapes=[
            pltpu.VMEM((7, *tile), jnp.float32),
            pltpu.VMEM((7, *tile), jnp.float32),
            pltpu.VMEM((3, *tile), jnp.float32),
            pltpu.VMEM(tile, jnp.float32),
            pltpu.VMEM(tile, jnp.float32),
            pltpu.SemaphoreType.DMA((17,)),
            pltpu.SemaphoreType.DMA((17,)),
        ],
        compiler_params=pltpu.CompilerParams(collective_id=1, has_side_effects=True),
        name="sum_scores",
    )(partial)


def on_device(sampled_rows, query_vectors, key_vectors):
    rows, all_heads, hd = query_vectors.shape
    groups = key_vectors.shape[1]
    heads = all_heads // groups
    q, k = gather(query_vectors.reshape(rows, groups, heads, hd), key_vectors.transpose(1, 2, 0))
    partial = compute(sampled_rows, q.reshape(-1, hd), k.reshape(-1, *k.shape[3:]), heads)
    return reduce(partial, 1.0 / heads).reshape(-1)


def solution(mesh):
    placed = (P(), P("seq", "kv", None), P("seq", "kv", None))
    return jax.shard_map(on_device, mesh=mesh, in_specs=placed, out_specs=P("seq"), check_vma=False)
```

```python
import functools
import math

import jax
import jax.numpy as jnp
from jax import lax
from jax.experimental import pallas as pl
from jax.experimental.pallas import tpu as pltpu
from jax.sharding import PartitionSpec as P

HD = 128
SCALE2 = math.log2(math.e) / math.sqrt(HD)
NEG = -1e30
BIG = 2.0**100
NZ, NX = 8, 4
MESH = pl.DeviceIdType.MESH
QB = 256
BLOCKS = 2
STEP = 8
MASKED = 4
DIRS = (1, -1)


def place():
    seq = lax.axis_index("seq")
    return lax.axis_index("kv"), seq // 8, lax.rem(seq // 2, 4), lax.rem(seq, 2)


def gather_kernel(q_ref, k_ref, qo_ref, ko_ref, lsem, ssem, rsem):
    y, z, x, c = place()
    head = lax.rem(z, 2)
    half = k_ref.shape[1] // 2

    def dev(zz, xx, cc):
        return (y, (zz * NX + xx) * 2 + cc)

    def zn(d):
        return lax.rem(z + d + NZ, NZ)

    def xn(d):
        return lax.rem(x + d + NX, NX)

    partner = dev(z, x, 1 - c)
    mirror = dev(NZ - 1 - z, x, c)
    barrier = pltpu.get_barrier_semaphore()
    peers = [partner, mirror]
    peers += [dev(zn(d), x, c) for d in (1, -1, 2, -2, 3, -3)]
    peers += [dev(z, xn(d), c) for d in DIRS]
    for p in peers:
        pl.semaphore_signal(barrier, inc=1, device_id=p, device_id_type=MESH)
    local_k = pltpu.make_async_copy(k_ref.at[head], ko_ref.at[z, x, c], lsem.at[0])
    local_k.start()
    local_q = pltpu.make_async_copy(q_ref.at[:, head], qo_ref.at[0], lsem.at[1])
    local_q.start()
    pl.semaphore_wait(barrier, len(peers))

    sends = []

    def send(src, dst, to):
        i = len(sends)
        cp = pltpu.make_async_remote_copy(
            src_ref=src, dst_ref=dst, send_sem=ssem.at[i], recv_sem=rsem.at[i], device_id=to, device_id_type=MESH
        )
        cp.start()
        sends.append(cp)
        return cp

    def block(zz, xx, piece=None):
        ref = ko_ref.at[zz, xx, c]
        return ref if piece is None else ref.at[pl.ds(piece * half, half)]

    def move(zz, xx, to, piece=None):
        r = block(zz, xx, piece)
        return send(r, r, to)

    mine = block(z, x)
    ax = {}
    az = {}
    for d in DIRS:
        az[d] = send(k_ref.at[1 - head], mine, dev(zn(d), x, c))
        ax[(0, d)] = send(k_ref.at[head], mine, dev(z, xn(d), c))
    for d in DIRS:
        az[2 * d] = send(k_ref.at[head], mine, dev(zn(2 * d), x, c))
    for d in DIRS:
        az[3 * d] = send(k_ref.at[1 - head], mine, dev(zn(3 * d), x, c))
    twin = [send(k_ref.at[head], mine, partner)]
    fx = {}

    def spread(zd):
        zz = zn(zd)
        for d in DIRS:
            ax[(zd, d)] = move(zz, x, dev(z, xn(d), c))
        twin.append(move(zz, x, partner))

    def forward(zd):
        zz = zn(zd)
        for d in DIRS:
            ax[(zd, d)].wait_recv()
        for d in DIRS:
            fx[(zd, d)] = move(zz, xn(-d), dev(z, xn(d), c), 0 if d == 1 else 1)
        for d in DIRS:
            twin.append(move(zz, xn(-d), partner))

    def finish(zd):
        for d in DIRS:
            fx[(zd, d)].wait_recv()
        twin.append(move(zn(zd), xn(2), partner))

    for d in DIRS:
        az[-d].wait_recv()
        spread(d)
    forward(0)
    for d in DIRS:
        az[-2 * d].wait_recv()
    far = {d: move(zn(2 * d), x, dev(zn(-2 * d), x, c), 0 if d == 1 else 1) for d in DIRS}
    for d in DIRS:
        spread(2 * d)
    swap = send(q_ref.at[:, 1 - head], qo_ref.at[1], mirror)
    for d in DIRS:
        forward(d)
    for d in DIRS:
        az[-3 * d].wait_recv()
        spread(3 * d)
    finish(0)
    for d in DIRS:
        forward(2 * d)
    for d in DIRS:
        far[d].wait_recv()
    spread(4)
    for d in DIRS:
        finish(d)
    for d in DIRS:
        forward(3 * d)
    for d in DIRS:
        finish(2 * d)
    forward(4)
    for d in DIRS:
        finish(3 * d)
    finish(4)
    local_k.wait()
    local_q.wait()
    swap.wait_recv()
    for cp in twin:
        cp.wait_recv()
    for cp in sends:
        cp.wait_send()


COPIES = 73


def gather(q, k):
    rows, _, heads, hd = q.shape
    return pl.pallas_call(
        gather_kernel,
        out_shape=(
            jax.ShapeDtypeStruct((2, rows, heads, hd), q.dtype),
            jax.ShapeDtypeStruct((NZ, NX, 2, *k.shape[1:]), k.dtype),
        ),
        in_specs=[pl.BlockSpec(memory_space=pltpu.HBM), pl.BlockSpec(memory_space=pl.ANY)],
        out_specs=(pl.BlockSpec(memory_space=pltpu.HBM),) * 2,
        scratch_shapes=[
            pltpu.SemaphoreType.DMA((2,)),
            pltpu.SemaphoreType.DMA((COPIES,)),
            pltpu.SemaphoreType.DMA((COPIES,)),
        ],
        compiler_params=pltpu.CompilerParams(collective_id=0, has_side_effects=True),
        name="gather_keys",
    )(q, k)


def compute_kernel(
    pos_hbm, q_hbm, k_hbm, out_ref, q_ref, k_ref, e_ref, acc_ref, m_ref, w_ref, z_ref, seen_ref, pos_ref, sems, *, heads
):
    _, z, x, c = place()
    all_rows = w_ref.shape[0]
    rows = all_rows // heads
    width = k_ref.shape[2]
    tiles = width // 128
    parts = all_rows // QB
    chunks = k_ref.shape[0] // STEP

    def fetch(step):
        r = pl.ds(step * STEP, STEP)
        return pltpu.make_async_copy(k_hbm.at[r], k_ref.at[r], sems.at[2 + step])

    fetch_pos = pltpu.make_async_copy(pos_hbm, pos_ref, sems.at[0])
    fetch_pos.start()
    fetch_q = pltpu.make_async_copy(q_hbm, q_ref, sems.at[1])
    fetch_q.start()
    for step in range(chunks):
        fetch(step).start()
    acc_ref[...] = jnp.zeros_like(acc_ref)
    fetch_pos.wait()
    fetch_q.wait()
    fetch(0).wait()
    iota = lax.broadcasted_iota(jnp.int32, (QB, 128), 1)

    def block(i, carry):
        plane = jnp.where(i < BLOCKS // 2, z, NZ - 1 - z)
        r0 = (((plane * NX + x) * 2 + c) * (BLOCKS // 2) + lax.rem(i, BLOCKS // 2)) * rows
        lo, hi = pos_ref[r0], pos_ref[r0 + rows - 1]
        open_end = (lo + 1) // (STEP * width)
        start_masked = open_end * (STEP // MASKED)
        end = hi // (MASKED * width) + 1
        for t in range(rows):
            seen_ref[t * heads : (t + 1) * heads] = jnp.full((heads, 128), pos_ref[r0 + t], jnp.int32)

        def queries(u):
            return q_ref[pl.ds(pl.multiple_of(i * all_rows + u * QB, QB), QB), :]

        for u in range(parts):
            r = slice(u * QB, (u + 1) * QB)
            first = jnp.dot(queries(u), k_ref[0, :, 0:128], preferred_element_type=jnp.float32)
            first = jnp.max(jnp.where(iota <= seen_ref[r], first, NEG), axis=1, keepdims=True)
            m_ref[r] = jnp.broadcast_to(first * SCALE2, (QB, 128))
        z_ref[...] = jnp.zeros_like(z_ref)

        def sweep(count, masked):
            def body(step, carry):
                if not masked:

                    @pl.when((i == 0) & (step > 0))
                    def _():
                        fetch(step).wait()

                for u in range(parts):
                    r = slice(u * QB, (u + 1) * QB)
                    qb = queries(u)
                    total = None
                    for g in range(count):
                        b = step * count + g
                        s = jnp.dot(qb, k_ref[b], preferred_element_type=jnp.float32)
                        for l in range(tiles):
                            e = jnp.exp2(s[:, l * 128 : (l + 1) * 128] * SCALE2 - m_ref[r])
                            if masked:
                                e = jnp.where(iota + (b * width + l * 128) <= seen_ref[r], e, 0.0)
                            e_ref[b * tiles + l, r] = e
                            total = e if total is None else total + e
                    z_ref[r] += total
                return carry

            return body

        lax.fori_loop(0, open_end, sweep(STEP, False), 0)

        @pl.when(i == 0)
        def _():
            def rest(step, carry):
                fetch(step).wait()
                return carry

            lax.fori_loop(jnp.maximum(open_end, 1), chunks, rest, 0)

        lax.fori_loop(start_masked, end, sweep(MASKED, True), 0)

        def weigh():
            total = jnp.sum(z_ref[...], axis=1, keepdims=True)
            w_ref[...] = jnp.broadcast_to(1.0 / total, w_ref.shape)
            return total

        total = weigh()

        @pl.when(jnp.logical_not(jnp.max(total) <= BIG))
        def _():
            for u in range(parts):
                r = slice(u * QB, (u + 1) * QB)
                qb = queries(u)

                def largest(b, best):
                    s = jnp.dot(qb, k_ref[b], preferred_element_type=jnp.float32)
                    for l in range(tiles):
                        seen = iota + (b * width + l * 128) <= seen_ref[r]
                        best = jnp.maximum(best, jnp.where(seen, s[:, l * 128 : (l + 1) * 128], NEG))
                    return best

                best = lax.fori_loop(0, end * MASKED, largest, jnp.full((QB, 128), NEG, jnp.float32))
                m_ref[r] = jnp.broadcast_to(jnp.max(best, axis=1, keepdims=True) * SCALE2, (QB, 128))
            z_ref[...] = jnp.zeros_like(z_ref)
            lax.fori_loop(0, end * MASKED, sweep(1, True), 0)
            weigh()

        def columns(step, carry):
            for g in range(0, MASKED * tiles, 4):
                b = step * (MASKED * tiles) + g
                sums = [acc_ref[b + l] for l in range(4)]
                for t in range(all_rows // 8):
                    weight = w_ref[8 * t : 8 * t + 8]
                    for l in range(4):
                        sums[l] = sums[l] + e_ref[b + l, 8 * t : 8 * t + 8, :] * weight
                for l in range(4):
                    acc_ref[b + l] = sums[l]
            return carry

        lax.fori_loop(0, end, columns, 0)
        return carry

    lax.fori_loop(0, BLOCKS, block, 0)
    for zz in range(8):
        for cc in range(2):
            for l in range(tiles):
                out_ref[zz, cc, :, l * 128 : (l + 1) * 128] = jnp.concatenate(
                    [
                        jnp.sum(acc_ref[((zz * NX + xx) * 2 + cc) * tiles + l], axis=0, keepdims=True)
                        for xx in range(NX)
                    ],
                    0,
                )


def compute(places, q, k, heads):
    blocks, _, width = k.shape
    rows = q.shape[0] // BLOCKS
    row = pltpu.VMEM((rows, 128), jnp.float32)
    return pl.pallas_call(
        functools.partial(compute_kernel, heads=heads),
        out_shape=jax.ShapeDtypeStruct((8, 2, NX, width), jnp.float32),
        in_specs=[pl.BlockSpec(memory_space=pltpu.HBM)] * 3,
        out_specs=pl.BlockSpec(memory_space=pltpu.VMEM),
        scratch_shapes=[
            pltpu.VMEM(q.shape, q.dtype),
            pltpu.VMEM(k.shape, k.dtype),
            pltpu.VMEM((blocks * width // 128, rows, 128), jnp.float32),
            pltpu.VMEM((blocks * width // 128, 8, 128), jnp.float32),
            row,
            row,
            row,
            pltpu.VMEM((rows, 128), jnp.int32),
            pltpu.SMEM(places.shape, jnp.int32),
            pltpu.SemaphoreType.DMA((2 + blocks // STEP,)),
        ],
        compiler_params=pltpu.CompilerParams(vmem_limit_bytes=60 << 20),
        name="key_scores",
    )(places, q, k)


def reduce_kernel(p_ref, out_ref, own, b1, b2, rows, lsem, ssem, rsem, *, factor):
    y, z, x, c = place()

    def dev(yy, zz, xx, cc):
        return (yy, (zz * NX + xx) * 2 + cc)

    def turn(i, d, n):
        return lax.rem(i + d, n)

    first = [(turn(z, d, 8), turn(c, e, 2)) for e in range(2) for d in range(8) if d or e]
    second = [(turn(x, d, 4), turn(y, e, 4)) for e in range(4) for d in range(4) if d or e]
    barrier = pltpu.get_barrier_semaphore()
    for zz, cc in first:
        pl.semaphore_signal(barrier, inc=1, device_id=dev(y, zz, x, cc), device_id_type=MESH)
    for xx, yy in second:
        pl.semaphore_signal(barrier, inc=1, device_id=dev(yy, z, xx, c), device_id_type=MESH)
    keep = pltpu.make_async_copy(p_ref.at[z, c], own, lsem)
    keep.start()
    pl.semaphore_wait(barrier, 30)
    cps = []

    def send(src, dst, to):
        i = len(cps)
        cp = pltpu.make_async_remote_copy(
            src_ref=src, dst_ref=dst, send_sem=ssem.at[i], recv_sem=rsem.at[i], device_id=to, device_id_type=MESH
        )
        cp.start()
        cps.append(cp)

    for i, (zz, cc) in enumerate(first):
        send(p_ref.at[zz, cc], b1.at[i], dev(y, zz, x, cc))
    keep.wait()
    total = own[...]
    for i in range(15):
        cps[i].wait_recv()
        total = total + b1[i]
    for r in range(4):
        rows[r] = total[r : r + 1]
    for i, (xx, yy) in enumerate(second):
        send(rows.at[xx], b2.at[i], dev(yy, z, xx, c))
    total = rows[x]
    for i in range(15):
        cps[15 + i].wait_recv()
        total = total + b2[i]
    out_ref[...] = total * factor
    for cp in cps:
        cp.wait_send()


def reduce(partial, factor):
    tile = partial.shape[2:]
    return pl.pallas_call(
        functools.partial(reduce_kernel, factor=factor),
        out_shape=jax.ShapeDtypeStruct((1, tile[1]), jnp.float32),
        in_specs=[pl.BlockSpec(memory_space=pl.ANY)],
        out_specs=pl.BlockSpec(memory_space=pltpu.VMEM),
        scratch_shapes=[
            pltpu.VMEM(tile, jnp.float32),
            pltpu.VMEM((15, *tile), jnp.float32),
            pltpu.VMEM((15, 1, tile[1]), jnp.float32),
            pltpu.VMEM((4, 1, tile[1]), jnp.float32),
            pltpu.SemaphoreType.DMA,
            pltpu.SemaphoreType.DMA((30,)),
            pltpu.SemaphoreType.DMA((30,)),
        ],
        compiler_params=pltpu.CompilerParams(collective_id=1, has_side_effects=True),
        name="sum_scores",
    )(partial)


def on_device(sampled_rows, query_vectors, key_vectors):
    rows, all_heads, hd = query_vectors.shape
    groups = key_vectors.shape[1]
    heads = all_heads // groups
    q, k = gather(query_vectors.reshape(rows, groups, heads, hd), key_vectors.transpose(1, 2, 0))
    partial = compute(sampled_rows, q.reshape(-1, hd), k.reshape(-1, *k.shape[3:]), heads)
    return reduce(partial, 1.0 / heads).reshape(-1)


def solution(mesh):
    placed = (P(), P("seq", "kv", None), P("seq", "kv", None))
    return jax.shard_map(on_device, mesh=mesh, in_specs=placed, out_specs=P("seq"), check_vma=False)
```

```python
import functools
import math

import jax
import jax.numpy as jnp
from jax import lax
from jax.experimental import pallas as pl
from jax.experimental.pallas import tpu as pltpu
from jax.sharding import PartitionSpec as P

HD = 128
SCALE2 = math.log2(math.e) / math.sqrt(HD)
NEG = -1e30
BIG = 2.0**100
NZ, NX = 8, 4
MESH = pl.DeviceIdType.MESH
QB = 256
BLOCKS = 2
STEP = 8
MASKED = 4
DIRS = (1, -1)


def place():
    seq = lax.axis_index("seq")
    return lax.axis_index("kv"), seq // 8, lax.rem(seq // 2, 4), lax.rem(seq, 2)


DOUBLE = (4,)

def gather_kernel(q_ref, k_ref, qo_ref, ko_ref, held, lsem, ssem, rsem):
    y, z, x, c = place()
    head = lax.rem(z, 2)
    half = k_ref.shape[1] // 2

    def dev(zz, xx, cc):
        return (y, (zz * NX + xx) * 2 + cc)

    def zn(d):
        return lax.rem(z + d + NZ, NZ)

    def xn(d):
        return lax.rem(x + d + NX, NX)

    partner = dev(z, x, 1 - c)
    mirror = dev(NZ - 1 - z, x, 1 - c)
    barrier = pltpu.get_barrier_semaphore()
    peers = [partner, mirror]
    peers += [dev(zn(d), x, c) for d in (1, -1, 2, -2)]
    peers += [dev(z, xn(d), cc) for d in DIRS for cc in (c, 1 - c)]
    for p in peers:
        pl.semaphore_signal(barrier, inc=1, device_id=p, device_id_type=MESH)
    local_k = pltpu.make_async_copy(k_ref.at[head], held.at[z, x, c], lsem.at[0])
    local_k.start()
    local_q = pltpu.make_async_copy(q_ref.at[:, head], qo_ref.at[0], lsem.at[1])
    local_q.start()
    pl.semaphore_wait(barrier, len(peers))

    sends = []

    def send(src, dst, to):
        i = len(sends)
        cp = pltpu.make_async_remote_copy(
            src_ref=src, dst_ref=dst, send_sem=ssem.at[i], recv_sem=rsem.at[i], device_id=to, device_id_type=MESH
        )
        cp.start()
        sends.append(cp)
        return cp

    def block(zz, xx, piece=None):
        ref = held.at[zz, xx, c]
        return ref if piece is None else ref.at[pl.ds(piece * half, half)]

    def move(zz, xx, to, piece=None):
        r = block(zz, xx, piece)
        return send(r, r, to)

    mine = block(z, x)
    ax = {}
    az = {}
    for d in DIRS:
        az[d] = send(k_ref.at[1 - head], mine, dev(zn(d), x, c))
        ax[(0, d)] = send(k_ref.at[head], mine, dev(z, xn(d), c))
    for d in DIRS:
        az[2 * d] = send(k_ref.at[head], mine, dev(zn(2 * d), x, c))
    twin = {zd: [] for zd in range(-3, 5)}
    twin[0].append(send(k_ref.at[head], mine, partner))
    fx = {}
    outs = []

    def write(zd, cc):
        zz = zn(zd)
        cp = pltpu.make_async_copy(held.at[zz, :, cc], ko_ref.at[zz, :, cc], lsem.at[2 + len(outs)])
        cp.start()
        outs.append(cp)

    def write_twin(zd):
        for cp in twin[zd]:
            cp.wait_recv()
        write(zd, 1 - c)

    def spread(zd):
        zz = zn(zd)
        for d in DIRS:
            ax[(zd, d)] = move(zz, x, dev(z, xn(d), c))
        twin[zd].append(move(zz, x, partner))

    def forward(zd):
        zz = zn(zd)
        for d in DIRS:
            ax[(zd, d)].wait_recv()
        for d in DIRS:
            fx[(zd, d)] = move(zz, xn(-d), dev(z, xn(d), c), 0 if d == 1 else 1)
        if zd in DOUBLE:
            for d in DIRS:
                twin[zd].append(move(zz, xn(-d), dev(z, xn(d), 1 - c), 0 if d == 1 else 1))
        for d in DIRS:
            twin[zd].append(move(zz, xn(-d), partner))

    def finish(zd):
        for d in DIRS:
            fx[(zd, d)].wait_recv()
        if zd not in DOUBLE:
            twin[zd].append(move(zn(zd), xn(2), partner))
        write(zd, c)

    for d in DIRS:
        az[d].wait_recv()
        az[3 * d] = move(zn(-d), x, dev(zn(2 * d), x, c))
        spread(-d)
    forward(0)
    for d in DIRS:
        az[-2 * d].wait_recv()
    far = {d: move(zn(2 * d), x, dev(zn(-2 * d), x, c), 0 if d == 1 else 1) for d in DIRS}
    for d in DIRS:
        spread(2 * d)
    for d in DIRS:
        forward(d)
    for d in DIRS:
        az[-3 * d].wait_recv()
        spread(3 * d)
    swap = send(q_ref.at[:, 1 - head], qo_ref.at[1], mirror)
    local_k.wait()
    finish(0)
    for d in DIRS:
        forward(2 * d)
    for d in DIRS:
        far[d].wait_recv()
    spread(4)
    for d in DIRS:
        finish(d)
    for d in DIRS:
        forward(3 * d)
    for d in DIRS:
        finish(2 * d)
    forward(4)
    for d in DIRS:
        finish(3 * d)
    for zd in (0, 1, -1, 2, -2):
        write_twin(zd)
    finish(4)
    for zd in (3, -3, 4):
        write_twin(zd)
    local_q.wait()
    swap.wait_recv()
    for cp in outs:
        cp.wait()
    for cp in sends:
        cp.wait_send()


COPIES = 74


def gather(q, k):
    rows, _, heads, hd = q.shape
    return pl.pallas_call(
        gather_kernel,
        out_shape=(
            jax.ShapeDtypeStruct((2, rows, heads, hd), q.dtype),
            jax.ShapeDtypeStruct((NZ, NX, 2, *k.shape[1:]), k.dtype),
        ),
        in_specs=[pl.BlockSpec(memory_space=pltpu.HBM), pl.BlockSpec(memory_space=pl.ANY)],
        out_specs=(pl.BlockSpec(memory_space=pltpu.HBM),) * 2,
        scratch_shapes=[
            pltpu.VMEM((NZ, NX, 2, *k.shape[1:]), k.dtype),
            pltpu.SemaphoreType.DMA((2 + 2 * NZ,)),
            pltpu.SemaphoreType.DMA((COPIES,)),
            pltpu.SemaphoreType.DMA((COPIES,)),
        ],
        compiler_params=pltpu.CompilerParams(collective_id=0, has_side_effects=True, vmem_limit_bytes=60 << 20),
        name="gather_keys",
    )(q, k)


def compute_kernel(
    pos_hbm, q_hbm, k_hbm, out_ref, q_ref, k_ref, e_ref, acc_ref, m_ref, w_ref, z_ref, seen_ref, pos_ref, sems, *, heads
):
    _, z, x, c = place()
    all_rows = w_ref.shape[0]
    rows = all_rows // heads
    width = k_ref.shape[2]
    tiles = width // 128
    parts = all_rows // QB
    chunks = k_ref.shape[0] // STEP

    def fetch(step):
        r = pl.ds(step * STEP, STEP)
        return pltpu.make_async_copy(k_hbm.at[r], k_ref.at[r], sems.at[2 + step])

    fetch_pos = pltpu.make_async_copy(pos_hbm, pos_ref, sems.at[0])
    fetch_pos.start()
    fetch_q = pltpu.make_async_copy(q_hbm, q_ref, sems.at[1])
    fetch_q.start()
    for step in range(chunks):
        fetch(step).start()
    acc_ref[...] = jnp.zeros_like(acc_ref)
    fetch_pos.wait()
    fetch_q.wait()
    fetch(0).wait()
    iota = lax.broadcasted_iota(jnp.int32, (QB, 128), 1)

    def block(i, carry):
        plane = jnp.where(i < BLOCKS // 2, z, NZ - 1 - z)
        core = jnp.where(i < BLOCKS // 2, c, 1 - c)
        r0 = (((plane * NX + x) * 2 + core) * (BLOCKS // 2) + lax.rem(i, BLOCKS // 2)) * rows
        lo, hi = pos_ref[r0], pos_ref[r0 + rows - 1]
        open_end = (lo + 1) // (STEP * width)
        start_masked = open_end * (STEP // MASKED)
        end = hi // (MASKED * width) + 1
        for t in range(rows):
            seen_ref[t * heads : (t + 1) * heads] = jnp.full((heads, 128), pos_ref[r0 + t], jnp.int32)

        def queries(u):
            return q_ref[pl.ds(pl.multiple_of(i * all_rows + u * QB, QB), QB), :]

        for u in range(parts):
            r = slice(u * QB, (u + 1) * QB)
            first = jnp.dot(queries(u), k_ref[0, :, 0:128], preferred_element_type=jnp.float32)
            first = jnp.max(jnp.where(iota <= seen_ref[r], first, NEG), axis=1, keepdims=True)
            m_ref[r] = jnp.broadcast_to(first * SCALE2, (QB, 128))
        z_ref[...] = jnp.zeros_like(z_ref)

        def sweep(count, masked):
            def body(step, carry):
                if not masked:

                    @pl.when((i == 0) & (step > 0))
                    def _():
                        fetch(step).wait()

                for u in range(parts):
                    r = slice(u * QB, (u + 1) * QB)
                    qb = queries(u)
                    total = None
                    for g in range(count):
                        b = step * count + g
                        s = jnp.dot(qb, k_ref[b], preferred_element_type=jnp.float32)
                        for l in range(tiles):
                            e = jnp.exp2(s[:, l * 128 : (l + 1) * 128] * SCALE2 - m_ref[r])
                            if masked:
                                e = jnp.where(iota + (b * width + l * 128) <= seen_ref[r], e, 0.0)
                            e_ref[b * tiles + l, r] = e
                            total = e if total is None else total + e
                    z_ref[r] += total
                return carry

            return body

        lax.fori_loop(0, open_end, sweep(STEP, False), 0)

        @pl.when(i == 0)
        def _():
            def rest(step, carry):
                fetch(step).wait()
                return carry

            lax.fori_loop(jnp.maximum(open_end, 1), chunks, rest, 0)

        lax.fori_loop(start_masked, end, sweep(MASKED, True), 0)

        def weigh():
            total = jnp.sum(z_ref[...], axis=1, keepdims=True)
            w_ref[...] = jnp.broadcast_to(1.0 / total, w_ref.shape)
            return total

        total = weigh()

        @pl.when(jnp.logical_not(jnp.max(total) <= BIG))
        def _():
            for u in range(parts):
                r = slice(u * QB, (u + 1) * QB)
                qb = queries(u)

                def largest(b, best):
                    s = jnp.dot(qb, k_ref[b], preferred_element_type=jnp.float32)
                    for l in range(tiles):
                        seen = iota + (b * width + l * 128) <= seen_ref[r]
                        best = jnp.maximum(best, jnp.where(seen, s[:, l * 128 : (l + 1) * 128], NEG))
                    return best

                best = lax.fori_loop(0, end * MASKED, largest, jnp.full((QB, 128), NEG, jnp.float32))
                m_ref[r] = jnp.broadcast_to(jnp.max(best, axis=1, keepdims=True) * SCALE2, (QB, 128))
            z_ref[...] = jnp.zeros_like(z_ref)
            lax.fori_loop(0, end * MASKED, sweep(1, True), 0)
            weigh()

        def columns(step, carry):
            for g in range(0, MASKED * tiles, 4):
                b = step * (MASKED * tiles) + g
                sums = [acc_ref[b + l] for l in range(4)]
                for t in range(all_rows // 8):
                    weight = w_ref[8 * t : 8 * t + 8]
                    for l in range(4):
                        sums[l] = sums[l] + e_ref[b + l, 8 * t : 8 * t + 8, :] * weight
                for l in range(4):
                    acc_ref[b + l] = sums[l]
            return carry

        lax.fori_loop(0, end, columns, 0)
        return carry

    lax.fori_loop(0, BLOCKS, block, 0)
    for zz in range(8):
        for cc in range(2):
            for l in range(tiles):
                out_ref[zz, cc, :, l * 128 : (l + 1) * 128] = jnp.concatenate(
                    [
                        jnp.sum(acc_ref[((zz * NX + xx) * 2 + cc) * tiles + l], axis=0, keepdims=True)
                        for xx in range(NX)
                    ],
                    0,
                )


def compute(places, q, k, heads):
    blocks, _, width = k.shape
    rows = q.shape[0] // BLOCKS
    row = pltpu.VMEM((rows, 128), jnp.float32)
    return pl.pallas_call(
        functools.partial(compute_kernel, heads=heads),
        out_shape=jax.ShapeDtypeStruct((8, 2, NX, width), jnp.float32),
        in_specs=[pl.BlockSpec(memory_space=pltpu.HBM)] * 3,
        out_specs=pl.BlockSpec(memory_space=pltpu.VMEM),
        scratch_shapes=[
            pltpu.VMEM(q.shape, q.dtype),
            pltpu.VMEM(k.shape, k.dtype),
            pltpu.VMEM((blocks * width // 128, rows, 128), jnp.float32),
            pltpu.VMEM((blocks * width // 128, 8, 128), jnp.float32),
            row,
            row,
            row,
            pltpu.VMEM((rows, 128), jnp.int32),
            pltpu.SMEM(places.shape, jnp.int32),
            pltpu.SemaphoreType.DMA((2 + blocks // STEP,)),
        ],
        compiler_params=pltpu.CompilerParams(vmem_limit_bytes=60 << 20),
        name="key_scores",
    )(places, q, k)


def reduce_kernel(p_ref, out_ref, own, b1, b2, rows, lsem, ssem, rsem):
    y, z, x, c = place()

    def dev(yy, zz, xx, cc):
        return (yy, (zz * NX + xx) * 2 + cc)

    def turn(i, d, n):
        return lax.rem(i + d, n)

    first = [(turn(z, d, 8), turn(c, e, 2)) for e in range(2) for d in range(8) if d or e]
    second = [(turn(x, d, 4), turn(y, e, 4)) for e in range(4) for d in range(4) if d or e]
    barrier = pltpu.get_barrier_semaphore()
    for zz, cc in first:
        pl.semaphore_signal(barrier, inc=1, device_id=dev(y, zz, x, cc), device_id_type=MESH)
    for xx, yy in second:
        pl.semaphore_signal(barrier, inc=1, device_id=dev(yy, z, xx, c), device_id_type=MESH)
    keep = pltpu.make_async_copy(p_ref.at[z, c], own, lsem)
    keep.start()
    pl.semaphore_wait(barrier, 30)
    cps = []

    def send(src, dst, to):
        i = len(cps)
        cp = pltpu.make_async_remote_copy(
            src_ref=src, dst_ref=dst, send_sem=ssem.at[i], recv_sem=rsem.at[i], device_id=to, device_id_type=MESH
        )
        cp.start()
        cps.append(cp)

    for i, (zz, cc) in enumerate(first):
        send(p_ref.at[zz, cc], b1.at[i], dev(y, zz, x, cc))
    keep.wait()
    total = own[...]
    for i in range(15):
        cps[i].wait_recv()
        total = total + b1[i]
    for r in range(4):
        rows[r] = total[r : r + 1]
    for i, (xx, yy) in enumerate(second):
        send(rows.at[xx], b2.at[i], dev(yy, z, xx, c))
    total = rows[x]
    for i in range(15):
        cps[15 + i].wait_recv()
        total = total + b2[i]
    out_ref[...] = total
    for cp in cps:
        cp.wait_send()


def reduce(partial):
    tile = partial.shape[2:]
    return pl.pallas_call(
        reduce_kernel,
        out_shape=jax.ShapeDtypeStruct((1, tile[1]), jnp.float32),
        in_specs=[pl.BlockSpec(memory_space=pl.ANY)],
        out_specs=pl.BlockSpec(memory_space=pltpu.VMEM),
        scratch_shapes=[
            pltpu.VMEM(tile, jnp.float32),
            pltpu.VMEM((15, *tile), jnp.float32),
            pltpu.VMEM((15, 1, tile[1]), jnp.float32),
            pltpu.VMEM((4, 1, tile[1]), jnp.float32),
            pltpu.SemaphoreType.DMA,
            pltpu.SemaphoreType.DMA((30,)),
            pltpu.SemaphoreType.DMA((30,)),
        ],
        compiler_params=pltpu.CompilerParams(collective_id=1, has_side_effects=True),
        name="sum_scores",
    )(partial)


def on_device(sampled_rows, query_vectors, key_vectors):
    rows, all_heads, hd = query_vectors.shape
    groups = key_vectors.shape[1]
    heads = all_heads // groups
    q, k = gather(query_vectors.reshape(rows, groups, heads, hd), key_vectors.transpose(1, 2, 0))
    partial = compute(sampled_rows, q.reshape(-1, hd), k.reshape(-1, *k.shape[3:]), heads)
    return reduce(partial).reshape(-1) * (1.0 / heads)


def solution(mesh):
    placed = (P(), P("seq", "kv", None), P("seq", "kv", None))
    return jax.shard_map(on_device, mesh=mesh, in_specs=placed, out_specs=P("seq"), check_vma=False)
```

```python
import functools
import math

import jax
import jax.numpy as jnp
from jax import lax
from jax.experimental import pallas as pl
from jax.experimental.pallas import tpu as pltpu
from jax.sharding import PartitionSpec as P

HD = 128
SCALE2 = math.log2(math.e) / math.sqrt(HD)
NEG = -1e30
BIG = 2.0**100
NZ, NX = 8, 4
MESH = pl.DeviceIdType.MESH
QB = 256
BLOCKS = 2
STEP = 8
MASKED = 4
DIRS = (1, -1)


def place():
    seq = lax.axis_index("seq")
    return lax.axis_index("kv"), seq // 8, lax.rem(seq // 2, 4), lax.rem(seq, 2)


DOUBLE = (4,)

def gather_kernel(q_ref, raw_hbm, qo_ref, ko_ref, held, raw, k_ref, lsem, ssem, rsem):
    y, z, x, c = place()
    fetch = pltpu.make_async_copy(raw_hbm, raw, lsem.at[2 + 2 * NZ])
    fetch.start()
    head = lax.rem(z, 2)
    half = k_ref.shape[1] // 2

    def dev(zz, xx, cc):
        return (y, (zz * NX + xx) * 2 + cc)

    def zn(d):
        return lax.rem(z + d + NZ, NZ)

    def xn(d):
        return lax.rem(x + d + NX, NX)

    partner = dev(z, x, 1 - c)
    mirror = dev(NZ - 1 - z, x, 1 - c)
    barrier = pltpu.get_barrier_semaphore()
    peers = [partner, mirror]
    peers += [dev(zn(d), x, c) for d in (1, -1, 2, -2)]
    peers += [dev(z, xn(d), cc) for d in DIRS for cc in (c, 1 - c)]
    for p in peers:
        pl.semaphore_signal(barrier, inc=1, device_id=p, device_id_type=MESH)
    fetch.wait()
    for h in range(k_ref.shape[0]):
        k_ref[h] = jnp.transpose(raw[:, h, :])
    local_k = pltpu.make_async_copy(k_ref.at[head], held.at[z, x, c], lsem.at[0])
    local_k.start()
    local_q = pltpu.make_async_copy(q_ref.at[:, head], qo_ref.at[0], lsem.at[1])
    local_q.start()
    pl.semaphore_wait(barrier, len(peers))

    sends = []

    def send(src, dst, to):
        i = len(sends)
        cp = pltpu.make_async_remote_copy(
            src_ref=src, dst_ref=dst, send_sem=ssem.at[i], recv_sem=rsem.at[i], device_id=to, device_id_type=MESH
        )
        cp.start()
        sends.append(cp)
        return cp

    def block(zz, xx, piece=None):
        ref = held.at[zz, xx, c]
        return ref if piece is None else ref.at[pl.ds(piece * half, half)]

    def move(zz, xx, to, piece=None):
        r = block(zz, xx, piece)
        return send(r, r, to)

    mine = block(z, x)
    ax = {}
    az = {}
    for d in DIRS:
        az[d] = send(k_ref.at[1 - head], mine, dev(zn(d), x, c))
        ax[(0, d)] = send(k_ref.at[head], mine, dev(z, xn(d), c))
    for d in DIRS:
        az[2 * d] = send(k_ref.at[head], mine, dev(zn(2 * d), x, c))
    twin = {zd: [] for zd in range(-3, 5)}
    twin[0].append(send(k_ref.at[head], mine, partner))
    fx = {}
    outs = []

    def write(zd, cc):
        zz = zn(zd)
        cp = pltpu.make_async_copy(held.at[zz, :, cc], ko_ref.at[zz, :, cc], lsem.at[2 + len(outs)])
        cp.start()
        outs.append(cp)

    def write_twin(zd):
        for cp in twin[zd]:
            cp.wait_recv()
        write(zd, 1 - c)

    def spread(zd):
        zz = zn(zd)
        for d in DIRS:
            ax[(zd, d)] = move(zz, x, dev(z, xn(d), c))
        twin[zd].append(move(zz, x, partner))

    def forward(zd):
        zz = zn(zd)
        for d in DIRS:
            ax[(zd, d)].wait_recv()
        for d in DIRS:
            fx[(zd, d)] = move(zz, xn(-d), dev(z, xn(d), c), 0 if d == 1 else 1)
        if zd in DOUBLE:
            for d in DIRS:
                twin[zd].append(move(zz, xn(-d), dev(z, xn(d), 1 - c), 0 if d == 1 else 1))
        for d in DIRS:
            twin[zd].append(move(zz, xn(-d), partner))

    def finish(zd):
        for d in DIRS:
            fx[(zd, d)].wait_recv()
        if zd not in DOUBLE:
            twin[zd].append(move(zn(zd), xn(2), partner))
        write(zd, c)

    for d in DIRS:
        az[d].wait_recv()
        az[3 * d] = move(zn(-d), x, dev(zn(2 * d), x, c))
        spread(-d)
    forward(0)
    for d in DIRS:
        az[-2 * d].wait_recv()
    far = {d: move(zn(2 * d), x, dev(zn(-2 * d), x, c), 0 if d == 1 else 1) for d in DIRS}
    for d in DIRS:
        spread(2 * d)
    for d in DIRS:
        forward(d)
    for d in DIRS:
        az[-3 * d].wait_recv()
        spread(3 * d)
    swap = send(q_ref.at[:, 1 - head], qo_ref.at[1], mirror)
    local_k.wait()
    finish(0)
    for d in DIRS:
        forward(2 * d)
    for d in DIRS:
        far[d].wait_recv()
    spread(4)
    for d in DIRS:
        finish(d)
    for d in DIRS:
        forward(3 * d)
    for d in DIRS:
        finish(2 * d)
    forward(4)
    for d in DIRS:
        finish(3 * d)
    for zd in (0, 1, -1, 2, -2):
        write_twin(zd)
    finish(4)
    for zd in (3, -3, 4):
        write_twin(zd)
    local_q.wait()
    swap.wait_recv()
    for cp in outs:
        cp.wait()
    for cp in sends:
        cp.wait_send()


COPIES = 74


def gather(q, k):
    rows, _, heads, hd = q.shape
    return pl.pallas_call(
        gather_kernel,
        out_shape=(
            jax.ShapeDtypeStruct((2, rows, heads, hd), q.dtype),
            jax.ShapeDtypeStruct((NZ, NX, 2, k.shape[2], k.shape[0]), k.dtype),
        ),
        in_specs=[pl.BlockSpec(memory_space=pltpu.HBM), pl.BlockSpec(memory_space=pl.ANY)],
        out_specs=(pl.BlockSpec(memory_space=pltpu.HBM),) * 2,
        scratch_shapes=[
            pltpu.VMEM((NZ, NX, 2, k.shape[2], k.shape[0]), k.dtype),
            pltpu.VMEM(k.shape, k.dtype),
            pltpu.VMEM((k.shape[1], k.shape[2], k.shape[0]), k.dtype),
            pltpu.SemaphoreType.DMA((3 + 2 * NZ,)),
            pltpu.SemaphoreType.DMA((COPIES,)),
            pltpu.SemaphoreType.DMA((COPIES,)),
        ],
        compiler_params=pltpu.CompilerParams(collective_id=0, has_side_effects=True, vmem_limit_bytes=60 << 20),
        name="gather_keys",
    )(q, k)


def compute_kernel(
    pos_hbm, q_hbm, k_hbm, out_ref, q_ref, k_ref, e_ref, acc_ref, m_ref, w_ref, z_ref, seen_ref, pos_ref, sems, *, heads
):
    _, z, x, c = place()
    all_rows = w_ref.shape[0]
    rows = all_rows // heads
    width = k_ref.shape[2]
    tiles = width // 128
    parts = all_rows // QB
    chunks = k_ref.shape[0] // STEP

    def fetch(step):
        r = pl.ds(step * STEP, STEP)
        return pltpu.make_async_copy(k_hbm.at[r], k_ref.at[r], sems.at[2 + step])

    fetch_pos = pltpu.make_async_copy(pos_hbm, pos_ref, sems.at[0])
    fetch_pos.start()
    fetch_q = pltpu.make_async_copy(q_hbm, q_ref, sems.at[1])
    fetch_q.start()
    for step in range(chunks):
        fetch(step).start()
    acc_ref[...] = jnp.zeros_like(acc_ref)
    fetch_pos.wait()
    fetch_q.wait()
    fetch(0).wait()
    iota = lax.broadcasted_iota(jnp.int32, (QB, 128), 1)

    def block(i, carry):
        plane = jnp.where(i < BLOCKS // 2, z, NZ - 1 - z)
        core = jnp.where(i < BLOCKS // 2, c, 1 - c)
        r0 = (((plane * NX + x) * 2 + core) * (BLOCKS // 2) + lax.rem(i, BLOCKS // 2)) * rows
        lo, hi = pos_ref[r0], pos_ref[r0 + rows - 1]
        open_end = (lo + 1) // (STEP * width)
        start_masked = open_end * (STEP // MASKED)
        end = hi // (MASKED * width) + 1
        for t in range(rows):
            seen_ref[t * heads : (t + 1) * heads] = jnp.full((heads, 128), pos_ref[r0 + t], jnp.int32)

        def queries(u):
            return q_ref[pl.ds(pl.multiple_of(i * all_rows + u * QB, QB), QB), :]

        for u in range(parts):
            r = slice(u * QB, (u + 1) * QB)
            first = jnp.dot(queries(u), k_ref[0, :, 0:128], preferred_element_type=jnp.float32)
            first = jnp.max(jnp.where(iota <= seen_ref[r], first, NEG), axis=1, keepdims=True)
            m_ref[r] = jnp.broadcast_to(first * SCALE2, (QB, 128))
        z_ref[...] = jnp.zeros_like(z_ref)

        def sweep(count, masked):
            def body(step, carry):
                if not masked:

                    @pl.when((i == 0) & (step > 0))
                    def _():
                        fetch(step).wait()

                for u in range(parts):
                    r = slice(u * QB, (u + 1) * QB)
                    qb = queries(u)
                    total = None
                    for g in range(count):
                        b = step * count + g
                        s = jnp.dot(qb, k_ref[b], preferred_element_type=jnp.float32)
                        for l in range(tiles):
                            e = jnp.exp2(s[:, l * 128 : (l + 1) * 128] * SCALE2 - m_ref[r])
                            if masked:
                                e = jnp.where(iota + (b * width + l * 128) <= seen_ref[r], e, 0.0)
                            e_ref[b * tiles + l, r] = e
                            total = e if total is None else total + e
                    z_ref[r] += total
                return carry

            return body

        lax.fori_loop(0, open_end, sweep(STEP, False), 0)

        @pl.when(i == 0)
        def _():
            def rest(step, carry):
                fetch(step).wait()
                return carry

            lax.fori_loop(jnp.maximum(open_end, 1), chunks, rest, 0)

        lax.fori_loop(start_masked, end, sweep(MASKED, True), 0)

        def weigh():
            total = jnp.sum(z_ref[...], axis=1, keepdims=True)
            w_ref[...] = jnp.broadcast_to(1.0 / total, w_ref.shape)
            return total

        total = weigh()

        @pl.when(jnp.logical_not(jnp.max(total) <= BIG))
        def _():
            for u in range(parts):
                r = slice(u * QB, (u + 1) * QB)
                qb = queries(u)

                def largest(b, best):
                    s = jnp.dot(qb, k_ref[b], preferred_element_type=jnp.float32)
                    for l in range(tiles):
                        seen = iota + (b * width + l * 128) <= seen_ref[r]
                        best = jnp.maximum(best, jnp.where(seen, s[:, l * 128 : (l + 1) * 128], NEG))
                    return best

                best = lax.fori_loop(0, end * MASKED, largest, jnp.full((QB, 128), NEG, jnp.float32))
                m_ref[r] = jnp.broadcast_to(jnp.max(best, axis=1, keepdims=True) * SCALE2, (QB, 128))
            z_ref[...] = jnp.zeros_like(z_ref)
            lax.fori_loop(0, end * MASKED, sweep(1, True), 0)
            weigh()

        def columns(step, carry):
            for g in range(0, MASKED * tiles, 4):
                b = step * (MASKED * tiles) + g
                sums = [acc_ref[b + l] for l in range(4)]
                for t in range(all_rows // 8):
                    weight = w_ref[8 * t : 8 * t + 8]
                    for l in range(4):
                        sums[l] = sums[l] + e_ref[b + l, 8 * t : 8 * t + 8, :] * weight
                for l in range(4):
                    acc_ref[b + l] = sums[l]
            return carry

        lax.fori_loop(0, end, columns, 0)
        return carry

    lax.fori_loop(0, BLOCKS, block, 0)
    for zz in range(8):
        for cc in range(2):
            for l in range(tiles):
                out_ref[zz, cc, :, l * 128 : (l + 1) * 128] = jnp.concatenate(
                    [
                        jnp.sum(acc_ref[((zz * NX + xx) * 2 + cc) * tiles + l], axis=0, keepdims=True)
                        for xx in range(NX)
                    ],
                    0,
                )


def compute(places, q, k, heads):
    blocks, _, width = k.shape
    rows = q.shape[0] // BLOCKS
    row = pltpu.VMEM((rows, 128), jnp.float32)
    return pl.pallas_call(
        functools.partial(compute_kernel, heads=heads),
        out_shape=jax.ShapeDtypeStruct((8, 2, NX, width), jnp.float32),
        in_specs=[pl.BlockSpec(memory_space=pltpu.HBM)] * 3,
        out_specs=pl.BlockSpec(memory_space=pltpu.VMEM),
        scratch_shapes=[
            pltpu.VMEM(q.shape, q.dtype),
            pltpu.VMEM(k.shape, k.dtype),
            pltpu.VMEM((blocks * width // 128, rows, 128), jnp.float32),
            pltpu.VMEM((blocks * width // 128, 8, 128), jnp.float32),
            row,
            row,
            row,
            pltpu.VMEM((rows, 128), jnp.int32),
            pltpu.SMEM(places.shape, jnp.int32),
            pltpu.SemaphoreType.DMA((2 + blocks // STEP,)),
        ],
        compiler_params=pltpu.CompilerParams(vmem_limit_bytes=60 << 20),
        name="key_scores",
    )(places, q, k)


def reduce_kernel(p_ref, out_ref, own, b1, b2, rows, lsem, ssem, rsem):
    y, z, x, c = place()

    def dev(yy, zz, xx, cc):
        return (yy, (zz * NX + xx) * 2 + cc)

    def turn(i, d, n):
        return lax.rem(i + d, n)

    def hops(d, n):
        return min(d, n - d)

    steps = sorted(((d, e) for d in range(8) for e in range(2) if d or e), key=lambda s: -hops(s[0], 8) - s[1])
    first = [(turn(z, d, 8), turn(c, e, 2)) for d, e in steps]
    steps = sorted(
        ((d, e) for d in range(4) for e in range(4) if d or e), key=lambda s: -hops(s[0], 4) - hops(s[1], 4)
    )
    second = [(turn(x, d, 4), turn(y, e, 4)) for d, e in steps]
    barrier = pltpu.get_barrier_semaphore()
    for zz, cc in first:
        pl.semaphore_signal(barrier, inc=1, device_id=dev(y, zz, x, cc), device_id_type=MESH)
    for xx, yy in second:
        pl.semaphore_signal(barrier, inc=1, device_id=dev(yy, z, xx, c), device_id_type=MESH)
    keep = pltpu.make_async_copy(p_ref.at[z, c], own, lsem)
    keep.start()
    pl.semaphore_wait(barrier, 30)
    cps = []

    def send(src, dst, to):
        i = len(cps)
        cp = pltpu.make_async_remote_copy(
            src_ref=src, dst_ref=dst, send_sem=ssem.at[i], recv_sem=rsem.at[i], device_id=to, device_id_type=MESH
        )
        cp.start()
        cps.append(cp)

    for i, (zz, cc) in enumerate(first):
        send(p_ref.at[zz, cc], b1.at[i], dev(y, zz, x, cc))
    keep.wait()
    total = own[...]
    for i in range(15):
        cps[i].wait_recv()
        total = total + b1[i]
    for r in range(4):
        rows[r] = total[r : r + 1]
    for i, (xx, yy) in enumerate(second):
        send(rows.at[xx], b2.at[i], dev(yy, z, xx, c))
    total = rows[x]
    for i in range(15):
        cps[15 + i].wait_recv()
        total = total + b2[i]
    out_ref[...] = total
    for cp in cps:
        cp.wait_send()


def reduce(partial):
    tile = partial.shape[2:]
    return pl.pallas_call(
        reduce_kernel,
        out_shape=jax.ShapeDtypeStruct((1, tile[1]), jnp.float32),
        in_specs=[pl.BlockSpec(memory_space=pl.ANY)],
        out_specs=pl.BlockSpec(memory_space=pltpu.VMEM),
        scratch_shapes=[
            pltpu.VMEM(tile, jnp.float32),
            pltpu.VMEM((15, *tile), jnp.float32),
            pltpu.VMEM((15, 1, tile[1]), jnp.float32),
            pltpu.VMEM((4, 1, tile[1]), jnp.float32),
            pltpu.SemaphoreType.DMA,
            pltpu.SemaphoreType.DMA((30,)),
            pltpu.SemaphoreType.DMA((30,)),
        ],
        compiler_params=pltpu.CompilerParams(collective_id=1, has_side_effects=True),
        name="sum_scores",
    )(partial)


def on_device(sampled_rows, query_vectors, key_vectors):
    rows, all_heads, hd = query_vectors.shape
    groups = key_vectors.shape[1]
    heads = all_heads // groups
    q, k = gather(query_vectors.reshape(rows, groups, heads, hd), key_vectors)
    partial = compute(sampled_rows, q.reshape(-1, hd), k.reshape(-1, *k.shape[3:]), heads)
    return reduce(partial).reshape(-1) * (1.0 / heads)


def solution(mesh):
    placed = (P(), P("seq", "kv", None), P("seq", "kv", None))
    return jax.shard_map(on_device, mesh=mesh, in_specs=placed, out_specs=P("seq"), check_vma=False)
```

```python
import functools
import math

import jax
import jax.numpy as jnp
from jax import lax
from jax.experimental import pallas as pl
from jax.experimental.pallas import tpu as pltpu
from jax.sharding import PartitionSpec as P

HD = 128
SCALE2 = math.log2(math.e) / math.sqrt(HD)
NEG = -1e30
BIG = 2.0**100
NZ, NX = 8, 4
MESH = pl.DeviceIdType.MESH
QB = 256
BLOCKS = 2
STEP = 8
MASKED = 4
DIRS = (1, -1)


def place():
    seq = lax.axis_index("seq")
    return lax.axis_index("kv"), seq // 8, lax.rem(seq // 2, 4), lax.rem(seq, 2)


DOUBLE = (4,)

def gather_kernel(q_ref, raw_hbm, qo_ref, ko_ref, held, raw, k_ref, lsem, ssem, rsem):
    y, z, x, c = place()
    fetch = pltpu.make_async_copy(raw_hbm, raw, lsem.at[2 + 2 * NZ])
    fetch.start()
    head = lax.rem(z, 2)
    half = k_ref.shape[1] // 2

    def dev(zz, xx, cc):
        return (y, (zz * NX + xx) * 2 + cc)

    def zn(d):
        return lax.rem(z + d + NZ, NZ)

    def xn(d):
        return lax.rem(x + d + NX, NX)

    partner = dev(z, x, 1 - c)
    mirror = dev(NZ - 1 - z, x, 1 - c)
    barrier = pltpu.get_barrier_semaphore()
    peers = [partner, mirror]
    peers += [dev(zn(d), x, c) for d in (1, -1, 2, -2)]
    peers += [dev(z, xn(d), cc) for d in DIRS for cc in (c, 1 - c)]
    for p in peers:
        pl.semaphore_signal(barrier, inc=1, device_id=p, device_id_type=MESH)
    fetch.wait()
    for h in range(k_ref.shape[0]):
        k_ref[h] = jnp.transpose(raw[:, h, :])
    local_k = pltpu.make_async_copy(k_ref.at[head], held.at[z, x, c], lsem.at[0])
    local_k.start()
    local_q = pltpu.make_async_copy(q_ref.at[:, head], qo_ref.at[0], lsem.at[1])
    local_q.start()
    pl.semaphore_wait(barrier, len(peers))

    sends = []

    def send(src, dst, to):
        i = len(sends)
        cp = pltpu.make_async_remote_copy(
            src_ref=src, dst_ref=dst, send_sem=ssem.at[i], recv_sem=rsem.at[i], device_id=to, device_id_type=MESH
        )
        cp.start()
        sends.append(cp)
        return cp

    def block(zz, xx, piece=None):
        ref = held.at[zz, xx, c]
        return ref if piece is None else ref.at[pl.ds(piece * half, half)]

    def move(zz, xx, to, piece=None):
        r = block(zz, xx, piece)
        return send(r, r, to)

    mine = block(z, x)
    ax = {}
    az = {}
    for d in DIRS:
        az[d] = send(k_ref.at[1 - head], mine, dev(zn(d), x, c))
        ax[(0, d)] = send(k_ref.at[head], mine, dev(z, xn(d), c))
    for d in DIRS:
        az[2 * d] = send(k_ref.at[head], mine, dev(zn(2 * d), x, c))
    twin = {zd: [] for zd in range(-3, 5)}
    twin[0].append(send(k_ref.at[head], mine, partner))
    fx = {}
    outs = []

    def write(zd, cc):
        zz = zn(zd)
        cp = pltpu.make_async_copy(held.at[zz, :, cc], ko_ref.at[zz, :, cc], lsem.at[2 + len(outs)])
        cp.start()
        outs.append(cp)

    def write_twin(zd):
        for cp in twin[zd]:
            cp.wait_recv()
        write(zd, 1 - c)

    def spread(zd):
        zz = zn(zd)
        for d in DIRS:
            ax[(zd, d)] = move(zz, x, dev(z, xn(d), c))
        twin[zd].append(move(zz, x, partner))

    def forward(zd):
        zz = zn(zd)
        for d in DIRS:
            ax[(zd, d)].wait_recv()
        for d in DIRS:
            fx[(zd, d)] = move(zz, xn(-d), dev(z, xn(d), c), 0 if d == 1 else 1)
        if zd in DOUBLE:
            for d in DIRS:
                twin[zd].append(move(zz, xn(-d), dev(z, xn(d), 1 - c), 0 if d == 1 else 1))
        for d in DIRS:
            twin[zd].append(move(zz, xn(-d), partner))

    def finish(zd):
        for d in DIRS:
            fx[(zd, d)].wait_recv()
        if zd not in DOUBLE:
            twin[zd].append(move(zn(zd), xn(2), partner))
        write(zd, c)

    for d in DIRS:
        az[d].wait_recv()
        az[3 * d] = move(zn(-d), x, dev(zn(2 * d), x, c))
        spread(-d)
    forward(0)
    for d in DIRS:
        az[-2 * d].wait_recv()
    far = {d: move(zn(2 * d), x, dev(zn(-2 * d), x, c), 0 if d == 1 else 1) for d in DIRS}
    for d in DIRS:
        spread(2 * d)
    for d in DIRS:
        forward(d)
    for d in DIRS:
        az[-3 * d].wait_recv()
        spread(3 * d)
    swap = send(q_ref.at[:, 1 - head], qo_ref.at[1], mirror)
    local_k.wait()
    finish(0)
    for d in DIRS:
        forward(2 * d)
    for d in DIRS:
        far[d].wait_recv()
    spread(4)
    for d in DIRS:
        finish(d)
    for d in DIRS:
        forward(3 * d)
    for d in DIRS:
        finish(2 * d)
    forward(4)
    for d in DIRS:
        finish(3 * d)
    for zd in (0, 1, -1, 2, -2):
        write_twin(zd)
    finish(4)
    for zd in (3, -3, 4):
        write_twin(zd)
    local_q.wait()
    swap.wait_recv()
    for cp in outs:
        cp.wait()
    for cp in sends:
        cp.wait_send()


COPIES = 74


def gather(q, k):
    rows, _, heads, hd = q.shape
    return pl.pallas_call(
        gather_kernel,
        out_shape=(
            jax.ShapeDtypeStruct((2, rows, heads, hd), q.dtype),
            jax.ShapeDtypeStruct((NZ, NX, 2, k.shape[2], k.shape[0]), k.dtype),
        ),
        in_specs=[pl.BlockSpec(memory_space=pltpu.HBM), pl.BlockSpec(memory_space=pl.ANY)],
        out_specs=(pl.BlockSpec(memory_space=pltpu.HBM),) * 2,
        scratch_shapes=[
            pltpu.VMEM((NZ, NX, 2, k.shape[2], k.shape[0]), k.dtype),
            pltpu.VMEM(k.shape, k.dtype),
            pltpu.VMEM((k.shape[1], k.shape[2], k.shape[0]), k.dtype),
            pltpu.SemaphoreType.DMA((3 + 2 * NZ,)),
            pltpu.SemaphoreType.DMA((COPIES,)),
            pltpu.SemaphoreType.DMA((COPIES,)),
        ],
        compiler_params=pltpu.CompilerParams(collective_id=0, has_side_effects=True, vmem_limit_bytes=60 << 20),
        name="gather_keys",
    )(q, k)


def compute_kernel(
    pos_hbm, q_hbm, k_hbm, out_ref, q_ref, k_ref, e_ref, acc_ref, m_ref, w_ref, z_ref, seen_ref, pos_ref, sems, *, heads
):
    _, z, x, c = place()
    all_rows = w_ref.shape[0]
    rows = all_rows // heads
    width = k_ref.shape[2]
    tiles = width // 128
    parts = all_rows // QB
    chunks = k_ref.shape[0] // STEP

    def fetch(step):
        r = pl.ds(step * STEP, STEP)
        return pltpu.make_async_copy(k_hbm.at[r], k_ref.at[r], sems.at[2 + step])

    fetch_pos = pltpu.make_async_copy(pos_hbm, pos_ref, sems.at[0])
    fetch_pos.start()
    fetch_q = pltpu.make_async_copy(q_hbm, q_ref, sems.at[1])
    fetch_q.start()
    for step in range(chunks):
        fetch(step).start()
    acc_ref[...] = jnp.zeros_like(acc_ref)
    fetch_pos.wait()
    fetch_q.wait()
    fetch(0).wait()
    iota = lax.broadcasted_iota(jnp.int32, (QB, 128), 1)

    def block(i, carry):
        plane = jnp.where(i < BLOCKS // 2, z, NZ - 1 - z)
        core = jnp.where(i < BLOCKS // 2, c, 1 - c)
        r0 = (((plane * NX + x) * 2 + core) * (BLOCKS // 2) + lax.rem(i, BLOCKS // 2)) * rows
        lo, hi = pos_ref[r0], pos_ref[r0 + rows - 1]
        open_end = (lo + 1) // (STEP * width)
        start_masked = open_end * (STEP // MASKED)
        end = hi // (MASKED * width) + 1
        for t in range(rows):
            seen_ref[t * heads : (t + 1) * heads] = jnp.full((heads, 128), pos_ref[r0 + t], jnp.int32)

        def queries(u):
            return q_ref[pl.ds(pl.multiple_of(i * all_rows + u * QB, QB), QB), :]

        for u in range(parts):
            r = slice(u * QB, (u + 1) * QB)
            first = jnp.dot(queries(u), k_ref[0, :, 0:128], preferred_element_type=jnp.float32)
            first = jnp.max(jnp.where(iota <= seen_ref[r], first, NEG), axis=1, keepdims=True)
            m_ref[r] = jnp.broadcast_to(first * SCALE2, (QB, 128))
        z_ref[...] = jnp.zeros_like(z_ref)

        def sweep(count, masked):
            def body(step, carry):
                if not masked:

                    @pl.when((i == 0) & (step > 0))
                    def _():
                        fetch(step).wait()

                for u in range(parts):
                    r = slice(u * QB, (u + 1) * QB)
                    qb = queries(u)
                    total = None
                    for g in range(count):
                        b = step * count + g
                        s = jnp.dot(qb, k_ref[b], preferred_element_type=jnp.float32)
                        for l in range(tiles):
                            e = jnp.exp2(s[:, l * 128 : (l + 1) * 128] * SCALE2 - m_ref[r])
                            if masked:
                                e = jnp.where(iota + (b * width + l * 128) <= seen_ref[r], e, 0.0)
                            e_ref[b * tiles + l, r] = e
                            total = e if total is None else total + e
                    z_ref[r] += total
                return carry

            return body

        lax.fori_loop(0, open_end, sweep(STEP, False), 0)

        @pl.when(i == 0)
        def _():
            def rest(step, carry):
                fetch(step).wait()
                return carry

            lax.fori_loop(jnp.maximum(open_end, 1), chunks, rest, 0)

        lax.fori_loop(start_masked, end, sweep(MASKED, True), 0)

        def weigh():
            total = jnp.sum(z_ref[...], axis=1, keepdims=True)
            w_ref[...] = jnp.broadcast_to(1.0 / total, w_ref.shape)
            return total

        total = weigh()

        @pl.when(jnp.logical_not(jnp.max(total) <= BIG))
        def _():
            for u in range(parts):
                r = slice(u * QB, (u + 1) * QB)
                qb = queries(u)

                def largest(b, best):
                    s = jnp.dot(qb, k_ref[b], preferred_element_type=jnp.float32)
                    for l in range(tiles):
                        seen = iota + (b * width + l * 128) <= seen_ref[r]
                        best = jnp.maximum(best, jnp.where(seen, s[:, l * 128 : (l + 1) * 128], NEG))
                    return best

                best = lax.fori_loop(0, end * MASKED, largest, jnp.full((QB, 128), NEG, jnp.float32))
                m_ref[r] = jnp.broadcast_to(jnp.max(best, axis=1, keepdims=True) * SCALE2, (QB, 128))
            z_ref[...] = jnp.zeros_like(z_ref)
            lax.fori_loop(0, end * MASKED, sweep(1, True), 0)
            weigh()

        def columns(step, carry):
            for g in range(0, MASKED * tiles, 4):
                b = step * (MASKED * tiles) + g
                sums = [acc_ref[b + l] for l in range(4)]
                for t in range(all_rows // 8):
                    weight = w_ref[8 * t : 8 * t + 8]
                    for l in range(4):
                        sums[l] = sums[l] + e_ref[b + l, 8 * t : 8 * t + 8, :] * weight
                for l in range(4):
                    acc_ref[b + l] = sums[l]
            return carry

        lax.fori_loop(0, end, columns, 0)
        return carry

    lax.fori_loop(0, BLOCKS, block, 0)
    for zz in range(8):
        for cc in range(2):
            for l in range(tiles):
                out_ref[zz, cc, :, l * 128 : (l + 1) * 128] = jnp.concatenate(
                    [
                        jnp.sum(acc_ref[((zz * NX + xx) * 2 + cc) * tiles + l], axis=0, keepdims=True)
                        for xx in range(NX)
                    ],
                    0,
                )


def compute(places, q, k, heads):
    blocks, _, width = k.shape
    rows = q.shape[0] // BLOCKS
    row = pltpu.VMEM((rows, 128), jnp.float32)
    return pl.pallas_call(
        functools.partial(compute_kernel, heads=heads),
        out_shape=jax.ShapeDtypeStruct((8, 2, NX, width), jnp.float32),
        in_specs=[pl.BlockSpec(memory_space=pltpu.HBM)] * 3,
        out_specs=pl.BlockSpec(memory_space=pltpu.VMEM),
        scratch_shapes=[
            pltpu.VMEM(q.shape, q.dtype),
            pltpu.VMEM(k.shape, k.dtype),
            pltpu.VMEM((blocks * width // 128, rows, 128), jnp.float32),
            pltpu.VMEM((blocks * width // 128, 8, 128), jnp.float32),
            row,
            row,
            row,
            pltpu.VMEM((rows, 128), jnp.int32),
            pltpu.SMEM(places.shape, jnp.int32),
            pltpu.SemaphoreType.DMA((2 + blocks // STEP,)),
        ],
        compiler_params=pltpu.CompilerParams(vmem_limit_bytes=60 << 20),
        name="key_scores",
    )(places, q, k)


def reduce_kernel(p_ref, out_ref, own, b1, b2, rows, lsem, ssem, rsem):
    y, z, x, c = place()

    def dev(yy, zz, xx, cc):
        return (yy, (zz * NX + xx) * 2 + cc)

    def turn(i, d, n):
        return lax.rem(i + d, n)

    def hops(d, n):
        return min(d, n - d)

    steps = sorted(((d, e) for d in range(8) for e in range(2) if d or e), key=lambda s: -hops(s[0], 8) - s[1])
    first = [(turn(z, d, 8), turn(c, e, 2)) for d, e in steps]
    steps = sorted(
        ((d, e) for d in range(4) for e in range(4) if d or e), key=lambda s: -hops(s[0], 4) - hops(s[1], 4)
    )
    second = [(turn(x, d, 4), turn(y, e, 4)) for d, e in steps]
    barrier = pltpu.get_barrier_semaphore()
    for zz, cc in first:
        pl.semaphore_signal(barrier, inc=1, device_id=dev(y, zz, x, cc), device_id_type=MESH)
    for xx, yy in second:
        pl.semaphore_signal(barrier, inc=1, device_id=dev(yy, z, xx, c), device_id_type=MESH)
    keep = pltpu.make_async_copy(p_ref.at[z, c], own, lsem)
    keep.start()
    pl.semaphore_wait(barrier, 30)
    cps = []

    def send(src, dst, to):
        i = len(cps)
        cp = pltpu.make_async_remote_copy(
            src_ref=src, dst_ref=dst, send_sem=ssem.at[i], recv_sem=rsem.at[i], device_id=to, device_id_type=MESH
        )
        cp.start()
        cps.append(cp)

    for i, (zz, cc) in enumerate(first):
        send(p_ref.at[zz, cc], b1.at[i], dev(y, zz, x, cc))
    keep.wait()
    total = own[...]
    for i in range(15):
        cps[i].wait_recv()
        total = total + b1[i]
    for r in range(4):
        rows[r] = total[r : r + 1]
    for i, (xx, yy) in enumerate(second):
        send(rows.at[xx], b2.at[i], dev(yy, z, xx, c))
    total = rows[x]
    for i in range(15):
        cps[15 + i].wait_recv()
        total = total + b2[i]
    out_ref[...] = total
    for cp in cps:
        cp.wait_send()


def reduce(partial):
    tile = partial.shape[2:]
    return pl.pallas_call(
        reduce_kernel,
        out_shape=jax.ShapeDtypeStruct((1, tile[1]), jnp.float32),
        in_specs=[pl.BlockSpec(memory_space=pl.ANY)],
        out_specs=pl.BlockSpec(memory_space=pltpu.VMEM),
        scratch_shapes=[
            pltpu.VMEM(tile, jnp.float32),
            pltpu.VMEM((15, *tile), jnp.float32),
            pltpu.VMEM((15, 1, tile[1]), jnp.float32),
            pltpu.VMEM((4, 1, tile[1]), jnp.float32),
            pltpu.SemaphoreType.DMA,
            pltpu.SemaphoreType.DMA((30,)),
            pltpu.SemaphoreType.DMA((30,)),
        ],
        compiler_params=pltpu.CompilerParams(collective_id=1, has_side_effects=True, vmem_limit_bytes=431 << 17),
        name="sum_scores",
    )(partial)


def on_device(sampled_rows, query_vectors, key_vectors):
    rows, all_heads, hd = query_vectors.shape
    groups = key_vectors.shape[1]
    heads = all_heads // groups
    q, k = gather(query_vectors.reshape(rows, groups, heads, hd), key_vectors)
    partial = compute(sampled_rows, q.reshape(-1, hd), k.reshape(-1, *k.shape[3:]), heads)
    return reduce(partial).reshape(-1) * (1.0 / heads)


def solution(mesh):
    placed = (P(), P("seq", "kv", None), P("seq", "kv", None))
    return jax.shard_map(on_device, mesh=mesh, in_specs=placed, out_specs=P("seq"), check_vma=False)
```

```python
import functools
import math

import jax
import jax.numpy as jnp
from jax import lax
from jax.experimental import pallas as pl
from jax.experimental.pallas import tpu as pltpu
from jax.sharding import PartitionSpec as P

HD = 128
SCALE2 = math.log2(math.e) / math.sqrt(HD)
NEG = -1e30
BIG = 2.0**100
NZ, NX = 8, 4
MESH = pl.DeviceIdType.MESH
QB = 256
BLOCKS = 2
STEP = 8
MASKED = 4
DIRS = (1, -1)


def place():
    seq = lax.axis_index("seq")
    return lax.axis_index("kv"), seq // 8, lax.rem(seq // 2, 4), lax.rem(seq, 2)


DOUBLE = (4,)

def gather_kernel(q_ref, raw_hbm, qo_ref, ko_ref, held, raw, k_ref, lsem, ssem, rsem):
    y, z, x, c = place()
    fetch = pltpu.make_async_copy(raw_hbm, raw, lsem.at[2 + 2 * NZ])
    fetch.start()
    head = lax.rem(z, 2)
    half = k_ref.shape[1] // 2

    def dev(zz, xx, cc):
        return (y, (zz * NX + xx) * 2 + cc)

    def zn(d):
        return lax.rem(z + d + NZ, NZ)

    def xn(d):
        return lax.rem(x + d + NX, NX)

    partner = dev(z, x, 1 - c)
    mirror = dev(NZ - 1 - z, x, 1 - c)
    barrier = pltpu.get_barrier_semaphore()
    peers = [partner, mirror]
    peers += [dev(zn(d), x, c) for d in (1, -1, 2, -2)]
    peers += [dev(z, xn(d), cc) for d in DIRS for cc in (c, 1 - c)]
    for p in peers:
        pl.semaphore_signal(barrier, inc=1, device_id=p, device_id_type=MESH)
    fetch.wait()
    for h in range(k_ref.shape[0]):
        k_ref[h] = jnp.transpose(raw[:, h, :])
    local_k = pltpu.make_async_copy(k_ref.at[head], held.at[z, x, c], lsem.at[0])
    local_k.start()
    local_q = pltpu.make_async_copy(q_ref.at[:, head], qo_ref.at[0], lsem.at[1])
    local_q.start()
    pl.semaphore_wait(barrier, len(peers))

    sends = []

    def send(src, dst, to):
        i = len(sends)
        cp = pltpu.make_async_remote_copy(
            src_ref=src, dst_ref=dst, send_sem=ssem.at[i], recv_sem=rsem.at[i], device_id=to, device_id_type=MESH
        )
        cp.start()
        sends.append(cp)
        return cp

    def block(zz, xx, piece=None):
        ref = held.at[zz, xx, c]
        return ref if piece is None else ref.at[pl.ds(piece * half, half)]

    def move(zz, xx, to, piece=None):
        r = block(zz, xx, piece)
        return send(r, r, to)

    mine = block(z, x)
    ax = {}
    az = {}
    for d in DIRS:
        az[d] = send(k_ref.at[1 - head], mine, dev(zn(d), x, c))
        ax[(0, d)] = send(k_ref.at[head], mine, dev(z, xn(d), c))
    for d in DIRS:
        az[2 * d] = send(k_ref.at[head], mine, dev(zn(2 * d), x, c))
    twin = {zd: [] for zd in range(-3, 5)}
    twin[0].append(send(k_ref.at[head], mine, partner))
    fx = {}
    outs = []

    def write(zd, cc):
        zz = zn(zd)
        cp = pltpu.make_async_copy(held.at[zz, :, cc], ko_ref.at[zz, :, cc], lsem.at[2 + len(outs)])
        cp.start()
        outs.append(cp)

    def write_twin(zd):
        for cp in twin[zd]:
            cp.wait_recv()
        write(zd, 1 - c)

    def spread(zd):
        zz = zn(zd)
        for d in DIRS:
            ax[(zd, d)] = move(zz, x, dev(z, xn(d), c))
        twin[zd].append(move(zz, x, partner))

    def forward(zd):
        zz = zn(zd)
        for d in DIRS:
            ax[(zd, d)].wait_recv()
        for d in DIRS:
            fx[(zd, d)] = move(zz, xn(-d), dev(z, xn(d), c), 0 if d == 1 else 1)
        if zd in DOUBLE:
            for d in DIRS:
                twin[zd].append(move(zz, xn(-d), dev(z, xn(d), 1 - c), 0 if d == 1 else 1))
        for d in DIRS:
            twin[zd].append(move(zz, xn(-d), partner))

    def finish(zd):
        for d in DIRS:
            fx[(zd, d)].wait_recv()
        if zd not in DOUBLE:
            twin[zd].append(move(zn(zd), xn(2), partner))
        write(zd, c)

    for d in DIRS:
        az[d].wait_recv()
        az[3 * d] = move(zn(-d), x, dev(zn(2 * d), x, c))
        spread(-d)
    forward(0)
    for d in DIRS:
        az[-2 * d].wait_recv()
    far = {d: move(zn(2 * d), x, dev(zn(-2 * d), x, c), 0 if d == 1 else 1) for d in DIRS}
    for d in DIRS:
        spread(2 * d)
    for d in DIRS:
        forward(d)
    for d in DIRS:
        az[-3 * d].wait_recv()
        spread(3 * d)
    swap = send(q_ref.at[:, 1 - head], qo_ref.at[1], mirror)
    local_k.wait()
    finish(0)
    for d in DIRS:
        forward(2 * d)
    for d in DIRS:
        far[d].wait_recv()
    spread(4)
    for d in DIRS:
        finish(d)
    for d in DIRS:
        forward(3 * d)
    for d in DIRS:
        finish(2 * d)
    forward(4)
    for d in DIRS:
        finish(3 * d)
    for zd in (0, 1, -1, 2, -2):
        write_twin(zd)
    finish(4)
    for zd in (3, -3, 4):
        write_twin(zd)
    local_q.wait()
    swap.wait_recv()
    for cp in outs:
        cp.wait()
    for cp in sends:
        cp.wait_send()


COPIES = 74


def gather(q, k):
    rows, _, heads, hd = q.shape
    return pl.pallas_call(
        gather_kernel,
        out_shape=(
            jax.ShapeDtypeStruct((2, rows, heads, hd), q.dtype),
            jax.ShapeDtypeStruct((NZ, NX, 2, k.shape[2], k.shape[0]), k.dtype),
        ),
        in_specs=[pl.BlockSpec(memory_space=pltpu.HBM), pl.BlockSpec(memory_space=pl.ANY)],
        out_specs=(pl.BlockSpec(memory_space=pltpu.HBM),) * 2,
        scratch_shapes=[
            pltpu.VMEM((NZ, NX, 2, k.shape[2], k.shape[0]), k.dtype),
            pltpu.VMEM(k.shape, k.dtype),
            pltpu.VMEM((k.shape[1], k.shape[2], k.shape[0]), k.dtype),
            pltpu.SemaphoreType.DMA((3 + 2 * NZ,)),
            pltpu.SemaphoreType.DMA((COPIES,)),
            pltpu.SemaphoreType.DMA((COPIES,)),
        ],
        compiler_params=pltpu.CompilerParams(collective_id=0, has_side_effects=True, vmem_limit_bytes=60 << 20),
        name="gather_keys",
    )(q, k)


def compute_kernel(
    pos_hbm, q_hbm, k_hbm, out_ref, q_ref, k_ref, e_ref, acc_ref, m_ref, w_ref, z_ref, seen_ref, pos_ref, sems, *, heads
):
    _, z, x, c = place()
    all_rows = w_ref.shape[0]
    rows = all_rows // heads
    width = k_ref.shape[2]
    tiles = width // 128
    parts = all_rows // QB
    chunks = k_ref.shape[0] // STEP

    def fetch(step):
        r = pl.ds(step * STEP, STEP)
        return pltpu.make_async_copy(k_hbm.at[r], k_ref.at[r], sems.at[2 + step])

    fetch_pos = pltpu.make_async_copy(pos_hbm, pos_ref, sems.at[0])
    fetch_pos.start()
    fetch_q = pltpu.make_async_copy(q_hbm, q_ref, sems.at[1])
    fetch_q.start()
    for step in range(chunks):
        fetch(step).start()
    acc_ref[...] = jnp.zeros_like(acc_ref)
    fetch_pos.wait()
    fetch_q.wait()
    fetch(0).wait()
    iota = lax.broadcasted_iota(jnp.int32, (QB, 128), 1)

    def block(i, carry):
        late = jnp.maximum(z, NZ - 1 - z)
        plane = jnp.where(i < BLOCKS // 2, late, NZ - 1 - late)
        own = plane == z
        core = jnp.where(own, c, 1 - c)
        slot = jnp.where(own, 0, BLOCKS // 2) + lax.rem(i, BLOCKS // 2)
        r0 = (((plane * NX + x) * 2 + core) * (BLOCKS // 2) + lax.rem(i, BLOCKS // 2)) * rows
        lo, hi = pos_ref[r0], pos_ref[r0 + rows - 1]
        open_end = (lo + 1) // (STEP * width)
        start_masked = open_end * (STEP // MASKED)
        end = hi // (MASKED * width) + 1
        for t in range(rows):
            seen_ref[t * heads : (t + 1) * heads] = jnp.full((heads, 128), pos_ref[r0 + t], jnp.int32)

        def queries(u):
            return q_ref[pl.ds(pl.multiple_of(slot * all_rows + u * QB, QB), QB), :]

        for u in range(parts):
            r = slice(u * QB, (u + 1) * QB)
            first = jnp.dot(queries(u), k_ref[0, :, 0:128], preferred_element_type=jnp.float32)
            first = jnp.max(jnp.where(iota <= seen_ref[r], first, NEG), axis=1, keepdims=True)
            m_ref[r] = jnp.broadcast_to(first * SCALE2, (QB, 128))
        z_ref[...] = jnp.zeros_like(z_ref)

        def sweep(count, masked):
            def body(step, carry):
                if not masked:

                    @pl.when((i == 0) & (step > 0))
                    def _():
                        fetch(step).wait()

                for u in range(parts):
                    r = slice(u * QB, (u + 1) * QB)
                    qb = queries(u)
                    total = None
                    for g in range(count):
                        b = step * count + g
                        s = jnp.dot(qb, k_ref[b], preferred_element_type=jnp.float32)
                        for l in range(tiles):
                            e = jnp.exp2(s[:, l * 128 : (l + 1) * 128] * SCALE2 - m_ref[r])
                            if masked:
                                e = jnp.where(iota + (b * width + l * 128) <= seen_ref[r], e, 0.0)
                            e_ref[b * tiles + l, r] = e
                            total = e if total is None else total + e
                    z_ref[r] += total
                return carry

            return body

        lax.fori_loop(0, open_end, sweep(STEP, False), 0)

        @pl.when(i == 0)
        def _():
            def rest(step, carry):
                fetch(step).wait()
                return carry

            lax.fori_loop(jnp.maximum(open_end, 1), chunks, rest, 0)

        lax.fori_loop(start_masked, end, sweep(MASKED, True), 0)

        def weigh():
            total = jnp.sum(z_ref[...], axis=1, keepdims=True)
            w_ref[...] = jnp.broadcast_to(1.0 / total, w_ref.shape)
            return total

        total = weigh()

        @pl.when(jnp.logical_not(jnp.max(total) <= BIG))
        def _():
            for u in range(parts):
                r = slice(u * QB, (u + 1) * QB)
                qb = queries(u)

                def largest(b, best):
                    s = jnp.dot(qb, k_ref[b], preferred_element_type=jnp.float32)
                    for l in range(tiles):
                        seen = iota + (b * width + l * 128) <= seen_ref[r]
                        best = jnp.maximum(best, jnp.where(seen, s[:, l * 128 : (l + 1) * 128], NEG))
                    return best

                best = lax.fori_loop(0, end * MASKED, largest, jnp.full((QB, 128), NEG, jnp.float32))
                m_ref[r] = jnp.broadcast_to(jnp.max(best, axis=1, keepdims=True) * SCALE2, (QB, 128))
            z_ref[...] = jnp.zeros_like(z_ref)
            lax.fori_loop(0, end * MASKED, sweep(1, True), 0)
            weigh()

        def columns(step, carry):
            for g in range(0, MASKED * tiles, 4):
                b = step * (MASKED * tiles) + g
                sums = [acc_ref[b + l] for l in range(4)]
                for t in range(all_rows // 8):
                    weight = w_ref[8 * t : 8 * t + 8]
                    for l in range(4):
                        sums[l] = sums[l] + e_ref[b + l, 8 * t : 8 * t + 8, :] * weight
                for l in range(4):
                    acc_ref[b + l] = sums[l]
            return carry

        lax.fori_loop(0, end, columns, 0)
        return carry

    lax.fori_loop(0, BLOCKS, block, 0)
    for zz in range(8):
        for cc in range(2):
            for l in range(tiles):
                out_ref[zz, cc, :, l * 128 : (l + 1) * 128] = jnp.concatenate(
                    [
                        jnp.sum(acc_ref[((zz * NX + xx) * 2 + cc) * tiles + l], axis=0, keepdims=True)
                        for xx in range(NX)
                    ],
                    0,
                )


def compute(places, q, k, heads):
    blocks, _, width = k.shape
    rows = q.shape[0] // BLOCKS
    row = pltpu.VMEM((rows, 128), jnp.float32)
    return pl.pallas_call(
        functools.partial(compute_kernel, heads=heads),
        out_shape=jax.ShapeDtypeStruct((8, 2, NX, width), jnp.float32),
        in_specs=[pl.BlockSpec(memory_space=pltpu.HBM)] * 3,
        out_specs=pl.BlockSpec(memory_space=pltpu.VMEM),
        scratch_shapes=[
            pltpu.VMEM(q.shape, q.dtype),
            pltpu.VMEM(k.shape, k.dtype),
            pltpu.VMEM((blocks * width // 128, rows, 128), jnp.float32),
            pltpu.VMEM((blocks * width // 128, 8, 128), jnp.float32),
            row,
            row,
            row,
            pltpu.VMEM((rows, 128), jnp.int32),
            pltpu.SMEM(places.shape, jnp.int32),
            pltpu.SemaphoreType.DMA((2 + blocks // STEP,)),
        ],
        compiler_params=pltpu.CompilerParams(vmem_limit_bytes=60 << 20),
        name="key_scores",
    )(places, q, k)


def reduce_kernel(p_ref, out_ref, own, b1, b2, rows, lsem, ssem, rsem):
    y, z, x, c = place()

    def dev(yy, zz, xx, cc):
        return (yy, (zz * NX + xx) * 2 + cc)

    def turn(i, d, n):
        return lax.rem(i + d, n)

    def hops(d, n):
        return min(d, n - d)

    steps = sorted(((d, e) for d in range(8) for e in range(2) if d or e), key=lambda s: -hops(s[0], 8) - s[1])
    first = [(turn(z, d, 8), turn(c, e, 2)) for d, e in steps]
    steps = sorted(
        ((d, e) for d in range(4) for e in range(4) if d or e), key=lambda s: -hops(s[0], 4) - hops(s[1], 4)
    )
    second = [(turn(x, d, 4), turn(y, e, 4)) for d, e in steps]
    barrier = pltpu.get_barrier_semaphore()
    for zz, cc in first:
        pl.semaphore_signal(barrier, inc=1, device_id=dev(y, zz, x, cc), device_id_type=MESH)
    for xx, yy in second:
        pl.semaphore_signal(barrier, inc=1, device_id=dev(yy, z, xx, c), device_id_type=MESH)
    keep = pltpu.make_async_copy(p_ref.at[z, c], own, lsem)
    keep.start()
    pl.semaphore_wait(barrier, 30)
    cps = []

    def send(src, dst, to):
        i = len(cps)
        cp = pltpu.make_async_remote_copy(
            src_ref=src, dst_ref=dst, send_sem=ssem.at[i], recv_sem=rsem.at[i], device_id=to, device_id_type=MESH
        )
        cp.start()
        cps.append(cp)

    for i, (zz, cc) in enumerate(first):
        send(p_ref.at[zz, cc], b1.at[i], dev(y, zz, x, cc))
    keep.wait()
    total = own[...]
    for i in range(15):
        cps[i].wait_recv()
        total = total + b1[i]
    for r in range(4):
        rows[r] = total[r : r + 1]
    for i, (xx, yy) in enumerate(second):
        send(rows.at[xx], b2.at[i], dev(yy, z, xx, c))
    total = rows[x]
    for i in range(15):
        cps[15 + i].wait_recv()
        total = total + b2[i]
    out_ref[...] = total
    for cp in cps:
        cp.wait_send()


def reduce(partial):
    tile = partial.shape[2:]
    return pl.pallas_call(
        reduce_kernel,
        out_shape=jax.ShapeDtypeStruct((1, tile[1]), jnp.float32),
        in_specs=[pl.BlockSpec(memory_space=pl.ANY)],
        out_specs=pl.BlockSpec(memory_space=pltpu.VMEM),
        scratch_shapes=[
            pltpu.VMEM(tile, jnp.float32),
            pltpu.VMEM((15, *tile), jnp.float32),
            pltpu.VMEM((15, 1, tile[1]), jnp.float32),
            pltpu.VMEM((4, 1, tile[1]), jnp.float32),
            pltpu.SemaphoreType.DMA,
            pltpu.SemaphoreType.DMA((30,)),
            pltpu.SemaphoreType.DMA((30,)),
        ],
        compiler_params=pltpu.CompilerParams(collective_id=1, has_side_effects=True, vmem_limit_bytes=431 << 17),
        name="sum_scores",
    )(partial)


def on_device(sampled_rows, query_vectors, key_vectors):
    rows, all_heads, hd = query_vectors.shape
    groups = key_vectors.shape[1]
    heads = all_heads // groups
    q, k = gather(query_vectors.reshape(rows, groups, heads, hd), key_vectors)
    partial = compute(sampled_rows, q.reshape(-1, hd), k.reshape(-1, *k.shape[3:]), heads)
    return reduce(partial).reshape(-1) * (1.0 / heads)


def solution(mesh):
    placed = (P(), P("seq", "kv", None), P("seq", "kv", None))
    return jax.shard_map(on_device, mesh=mesh, in_specs=placed, out_specs=P("seq"), check_vma=False)
```
